512 devices in a mesh: beam: 128 (over z, y, x_hi), grp: 4 (over x_lo, core).
Axes of the slice: x: 4 (x_hi: 2, x_lo: 2; x = x_hi * 2 + x_lo), y: 8, z: 8, core: 2. Of those that a mesh axis runs over, the one named last changes fastest.
Arguments:
- potential: bfloat16 [2, 262144], P(None, 'beam'), may hold values from -6 to 6
- wave_vectors: int32 [512, 2], replicated, may hold values from -64 to 63
- probe_sites: int32 [64, 2], replicated, may hold values from 0 to 511
Outputs:
- probe_waves: float32 [2, 64, 65536], P(None, 'grp', 'beam')
The draws below stay inside these ranges and needn't reach their ends.
All inputs are finite; a program needn't handle non-finite values.
Results may differ from the reference program's by a relative error of at most 0.012.
Values may be sent and summed in bfloat16 or wider, within the bound.
No kernel may reach another device: no remote copies, remote signals or barrier semaphores. Data moves between devices by JAX's collectives and lax.ppermute only.
A program may use at most 64 MiB of HBM per device.

```python
import math
import jax
import jax.numpy as jnp
from jax import lax

G = 512
BAND = 256
SLICES = 2
PROBES = 64
BEAMS = 512


def place_ends(array, own_key, low, top_value):
    extent = array.shape
    place = [jax.random.randint(jax.random.fold_in(own_key, axis), (), 0, extent[axis]) for axis in range(len(extent))]
    array = array.at[tuple(place)].set(low)
    longest = extent.index(max(extent))
    place[longest] = (place[longest] + 1) % extent[longest]
    return array.at[tuple(place)].set(top_value)


def shard_levels(own_key, shape, pieces, least, high):
    gain = 1.0
    for axis_at, blocks in pieces:
        heights = jax.random.uniform(jax.random.fold_in(jax.random.fold_in(own_key, 6), axis_at), (blocks,), jnp.float32, least / len(pieces), high / len(pieces))
        gain = gain * jnp.repeat(jnp.exp(heights), shape[axis_at] // blocks).reshape((-1,) + (1,) * (len(shape) - 1 - axis_at))
    return gain


def normal_values(own_key, extent, scale, most, split=(), kind=jnp.bfloat16):
    entries = scale * jax.random.normal(own_key, extent, jnp.float32)
    if split:
        entries = entries * shard_levels(own_key, extent, split, -0.22, 0.18)
    return jnp.clip(entries, -most, most).astype(kind)


def setup_inputs(seed: int = 0) -> dict:
    keys = jax.random.split(jax.random.key(seed), 4)
    return {
        "potential": normal_values(keys[0], (SLICES, G * G), 1.0, 6.0, ((1, 128),)),
        "wave_vectors": place_ends(jax.random.randint(keys[1], (BEAMS, 2), 0 - BAND // 4, BAND // 4), jax.random.fold_in(keys[1], 1), 0 - BAND // 4, (BAND // 4) - 1).astype(jnp.int32),
        "probe_sites": place_ends(jax.random.randint(keys[2], (PROBES, 2), 0, G), jax.random.fold_in(keys[2], 1), 0, G - 1).astype(jnp.int32),
    }


PHASE_SCALE = 2.5
CHIRP_RATE = 20
EXACT = lax.Precision.HIGHEST

def dft_table(freqs, places, length, sign):
    phases = jnp.mod(freqs[:, None] * places[None, :], length)
    angle = 2.0 * math.pi / length * phases.astype(jnp.float32)
    factor = 1.0 / math.sqrt(length)
    return ((jnp.cos(angle) * factor).astype(jnp.bfloat16), (sign * jnp.sin(angle) * factor).astype(jnp.bfloat16))

def propagator(freqs):
    squared = freqs[:, None] * freqs[:, None] + freqs[None, :] * freqs[None, :]
    inside = (9 * squared < G * G).astype(jnp.float32)
    chirp = jnp.mod(CHIRP_RATE * squared, G * G)
    angle = -2.0 * math.pi / (G * G) * chirp.astype(jnp.float32)
    return (inside * jnp.cos(angle), inside * jnp.sin(angle))

def rounded(pair):
    return (pair[0].astype(jnp.bfloat16), pair[1].astype(jnp.bfloat16))

def times(pair, other):
    return (pair[0] * other[0] - pair[1] * other[1], pair[0] * other[1] + pair[1] * other[0])

def left_exact(table, data):
    t_real, t_imag = (table[0].astype(jnp.float32), table[1].astype(jnp.float32))
    d_real, d_imag = (data[0].astype(jnp.float32), data[1].astype(jnp.float32))
    return (jnp.dot(t_real, d_real, precision=EXACT) - jnp.dot(t_imag, d_imag, precision=EXACT), jnp.dot(t_real, d_imag, precision=EXACT) + jnp.dot(t_imag, d_real, precision=EXACT))

def right_exact(data, table):
    t_real, t_imag = (table[0].astype(jnp.float32), table[1].astype(jnp.float32))
    d_real, d_imag = (data[0].astype(jnp.float32), data[1].astype(jnp.float32))
    return (jnp.dot(d_real, t_real, precision=EXACT) - jnp.dot(d_imag, t_imag, precision=EXACT), jnp.dot(d_real, t_imag, precision=EXACT) + jnp.dot(d_imag, t_real, precision=EXACT))

def transform(data, first, second):
    return right_exact(rounded(left_exact(first, data)), second)

def exit_wave(wave_x, wave_y, slabs):
    places = jnp.arange(G, dtype=jnp.int32)
    full_freqs = jnp.where(places < G // 2, places, places - G)
    band_freqs = jnp.arange(BAND, dtype=jnp.int32) - BAND // 2
    forward = dft_table(places, places, G, -1.0)
    inverse = dft_table(places, places, G, 1.0)
    crop_rows = dft_table(band_freqs, places, G, -1.0)
    crop_cols = (crop_rows[0].T, crop_rows[1].T)
    full_prop = propagator(full_freqs)
    band_prop = propagator(band_freqs)
    phases = jnp.mod(wave_x * places[:, None] + wave_y * places[None, :], G)
    angle = 2.0 * math.pi / G * phases.astype(jnp.float32)
    wave = (jnp.cos(angle), jnp.sin(angle))
    result = None
    for layer in range(SLICES):
        shift = PHASE_SCALE * slabs[layer].astype(jnp.float32)
        passed = rounded(times(wave, (jnp.cos(shift), jnp.sin(shift))))
        if layer + 1 < SLICES:
            spectrum = rounded(times(transform(passed, forward, forward), full_prop))
            wave = transform(spectrum, inverse, inverse)
        else:
            result = rounded(times(transform(passed, crop_rows, crop_cols), band_prop))
    return result

def coefficients(vectors, sites, count):
    wave_x = vectors[:, 0]
    wave_y = vectors[:, 1]
    phases = jnp.mod(sites[:, 0:1] * wave_x[None, :] + sites[:, 1:2] * wave_y[None, :], G)
    angle = -2.0 * math.pi / G * phases.astype(jnp.float32)
    weight = jnp.exp(-(wave_x * wave_x + wave_y * wave_y).astype(jnp.float32) * (8.0 / (BAND * BAND)))
    weight = weight[None, :] * (1.0 / math.sqrt(count))
    return ((weight * jnp.cos(angle)).astype(jnp.bfloat16), (weight * jnp.sin(angle)).astype(jnp.bfloat16))

def reference(potential, wave_vectors, probe_sites):
    slabs = potential.reshape(SLICES, G, G)

    def one_beam(vector):
        wave_real, wave_imag = exit_wave(vector[0], vector[1], slabs)
        return jnp.stack([wave_real.reshape(-1), wave_imag.reshape(-1)], 0)
    smatrix = lax.map(one_beam, wave_vectors)
    coef_real, coef_imag = coefficients(wave_vectors, probe_sites, BEAMS)
    coef_real = coef_real.astype(jnp.float32)
    coef_imag = coef_imag.astype(jnp.float32)
    s_real = smatrix[:, 0, :].astype(jnp.float32)
    s_imag = smatrix[:, 1, :].astype(jnp.float32)
    real = jnp.dot(coef_real, s_real, precision=EXACT) - jnp.dot(coef_imag, s_imag, precision=EXACT)
    imag = jnp.dot(coef_real, s_imag, precision=EXACT) + jnp.dot(coef_imag, s_real, precision=EXACT)
    return jnp.stack([real, imag], 0)
```

```python
import math

import jax
import jax.numpy as jnp
import numpy as np
from jax import lax
from jax.experimental import pallas as pl
from jax.experimental.pallas import tpu as pltpu
from jax.sharding import PartitionSpec as P

G = 512
BAND = 256
NQ = 384
PHASE_SCALE = 2.5
CHIRP_RATE = 20
BLOCK = 64
ROWS = 18

F32 = jnp.float32
BF16 = jnp.bfloat16


def frequencies():
    reach = math.isqrt((G * G - 1) // 9)
    band = np.arange(-BAND // 2, BAND // 2)
    high = np.arange(BAND // 2, reach + 1)
    low = np.arange(-reach, -BAND // 2)
    return np.concatenate([band, high, low])


def forward_table(places):
    freqs = frequencies()
    phases = np.mod(freqs[None, :] * places[:, None], G)
    angle = 2.0 * np.pi / G * phases
    table = np.zeros((2, places.shape[0], NQ), np.float64)
    table[0, :, : freqs.size] = np.cos(angle) / np.sqrt(G)
    table[1, :, : freqs.size] = -np.sin(angle) / np.sqrt(G)
    return table


def constant_tables():
    places = np.arange(G)
    permuted = (4 * np.arange(G // 4)[None, :] + np.arange(4)[:, None]).reshape(-1)
    natural = forward_table(places)
    shuffled = forward_table(permuted)
    right = np.concatenate([natural[0], natural[1]], 1)
    left = np.concatenate([shuffled[0].T, shuffled[1].T], 0)
    back = np.concatenate([shuffled[0], -shuffled[1]], 1)
    freqs = frequencies()
    squared = np.full((NQ,), 1.0e9)
    squared[: freqs.size] = freqs * freqs
    angle = np.zeros((NQ,))
    angle[: freqs.size] = -2.0 * np.pi / (G * G) * np.mod(CHIRP_RATE * freqs * freqs, G * G)
    chirp = np.stack([np.cos(angle), np.sin(angle), squared], 0)
    lanes = np.zeros((8, NQ))
    lanes[:3] = chirp
    return (
        right.astype(BF16),
        left.astype(BF16),
        back.astype(BF16),
        lanes.astype(np.float32),
    )


def half_turn_fits():
    nodes = 0.5 * np.cos(np.pi * (np.arange(400) + 0.5) / 400)
    square = nodes * nodes
    sine = np.polynomial.Polynomial.fit(square, np.sin(np.pi * nodes) / nodes, 4, domain=[0, 0.25])
    cosine = np.polynomial.Polynomial.fit(square, np.cos(np.pi * nodes), 4, domain=[0, 0.25])
    return (
        [float(v) for v in sine.convert().coef],
        [float(v) for v in cosine.convert().coef],
    )


SINE, COSINE = half_turn_fits()


def horner(coefs, x):
    total = coefs[-1]
    for coef in coefs[-2::-1]:
        total = total * x + coef
    return total


def phase_factor(cells):
    turns = cells * (PHASE_SCALE / (2.0 * math.pi))
    rest = turns - jnp.floor(turns + 0.5)
    square = rest * rest
    sine = rest * horner(SINE, square)
    cosine = horner(COSINE, square)
    return 1.0 - 2.0 * sine * sine, 2.0 * sine * cosine


def dot(a, b):
    return jnp.dot(a, b, preferred_element_type=F32)


def dot_t(a, b):
    return lax.dot_general(a, b, (((1,), (1,)), ((), ())), preferred_element_type=F32)


def prepare_kernel(place, beams, right, back, chirp, chirp_t, phi, inverse, prop, final):
    index = lax.broadcasted_iota(jnp.int32, (BAND, G), 0).astype(F32)
    on_x = index == beams[0:1, :]
    on_y = jnp.where(index == beams[1:2, :], 1.0, 0.0).astype(BF16)
    grid_r = dot_t(jnp.where(on_x, beams[2:3, :], 0.0).astype(BF16), on_y)
    grid_i = dot_t(jnp.where(on_x, beams[3:4, :], 0.0).astype(BF16), on_y)
    grid = jnp.concatenate([grid_r, grid_i], 1).astype(BF16)
    by_r = dot(back[:, 0:BAND], grid)
    by_i = dot(back[:, NQ : NQ + BAND], grid)
    mid_r = by_r[:, :BAND] - by_i[:, BAND:]
    mid_i = by_r[:, BAND:] + by_i[:, :BAND]
    band_r = right[:, 0:BAND]
    band_i = right[:, NQ : NQ + BAND]
    both = jnp.concatenate([band_r, band_i], 1)
    phi[:, :G] = dot_t(jnp.concatenate([mid_r, mid_i], 1).astype(BF16), both)
    phi[:, G:] = dot_t(jnp.concatenate([mid_i, -mid_r], 1).astype(BF16), both)
    start = pl.multiple_of(place[0] * BLOCK, BLOCK)
    own_r = right[pl.ds(start, BLOCK), 0:NQ]
    own_i = right[pl.ds(start, BLOCK), NQ:]
    inverse[0:64, :NQ] = own_r
    inverse[0:64, NQ:] = own_i
    inverse[64:128, :NQ] = -own_i
    inverse[64:128, NQ:] = own_r
    inverse[128:192, :NQ] = own_i
    inverse[128:192, NQ:] = -own_r
    inverse[192:256, :NQ] = own_r
    inverse[192:256, NQ:] = own_i
    inside = chirp_t[:, 2:3] + chirp[2:3, :] < (G * G - 1) // 9 + 0.5
    xr = chirp_t[:, 0:1]
    xi = chirp_t[:, 1:2]
    yr = chirp[0:1, :]
    yi = chirp[1:2, :]
    prop[:, :NQ] = jnp.where(inside, xr * yr - xi * yi, 0.0)
    prop[:, NQ:] = jnp.where(inside, xr * yi + xi * yr, 0.0)
    for k in range(G // BLOCK):
        rows = slice(k * BLOCK, (k + 1) * BLOCK)
        top = slice(2 * k * BLOCK, (2 * k + 1) * BLOCK)
        low = slice((2 * k + 1) * BLOCK, (2 * k + 2) * BLOCK)
        final[top, :BAND] = right[rows, 0:BAND]
        final[top, BAND:] = right[rows, NQ : NQ + BAND]
        final[low, :BAND] = -right[rows, NQ : NQ + BAND]
        final[low, BAND:] = right[rows, 0:BAND]


def main_kernel(cells, phi, right, left, back, inverse, prop, out, wide, data, half, spec, fold):
    wide[...] = cells[...].astype(F32)
    for j in range(4):
        rows = slice(128 * j, 128 * j + 128)
        for h in range(4):
            cols = slice(128 * h, 128 * h + 128)
            cos, sin = phase_factor(wide[pl.ds(4 * j + h, 128, stride=ROWS), :])
            pr = phi[rows, 128 * h : 128 * h + 128]
            pi = phi[rows, G + 128 * h : G + 128 * h + 128]
            data[rows, cols] = (pr * cos - pi * sin).astype(BF16)
            data[rows, G + 128 * h : G + 128 * h + 128] = (pr * sin + pi * cos).astype(BF16)
        one = dot(data[rows, :G], right[...])
        two = dot(data[rows, G:], right[...])
        half[rows, :NQ] = (one[:, :NQ] - two[:, NQ:]).astype(BF16)
        half[rows, NQ:] = (one[:, NQ:] + two[:, :NQ]).astype(BF16)
    for j in range(3):
        rows = slice(128 * j, 128 * j + 128)
        one = dot(left[rows, :], half[...])
        two = dot(left[NQ + 128 * j : NQ + 128 * j + 128, :], half[...])
        re = one[:, :NQ] - two[:, NQ:]
        im = one[:, NQ:] + two[:, :NQ]
        pr = prop[rows, :NQ]
        pi = prop[rows, NQ:]
        spec[rows, :NQ] = (re * pr - im * pi).astype(BF16)
        spec[rows, NQ:] = (re * pi + im * pr).astype(BF16)
        turned = dot_t(spec[rows, :], inverse[...])
        low = slice(NQ + 128 * j, NQ + 128 * j + 128)
        fold[rows, :] = turned.astype(BF16)
        fold[low, :128] = turned[:, 128:].astype(BF16)
        fold[low, 128:] = (-turned[:, :128]).astype(BF16)
    lane = lax.broadcasted_iota(jnp.int32, (128, 128), 1) < BLOCK
    for j in range(4):
        rows = slice(128 * j, 128 * j + 128)
        pair = wide[pl.ds(16 + j // 2, 128, stride=ROWS), :]
        other = pltpu.roll(pair, BLOCK, 1)
        own = jnp.where(lane, pair, other) if j % 2 == 0 else jnp.where(lane, other, pair)
        cos, sin = phase_factor(own)
        wave = dot(back[rows, :], fold[...])
        data[rows, :128] = (wave[:, :128] * cos + wave[:, 128:] * sin).astype(BF16)
        data[rows, 128:256] = (wave[:, 128:] * cos - wave[:, :128] * sin).astype(BF16)
    total = dot(left[0:BAND, :], data[:, :128]) + dot(left[NQ : NQ + BAND, :], data[:, 128:256])
    out[...] = total.astype(BF16)


def final_kernel(parts, final, prop, out, total):
    acc = dot(parts[0:32, :], final[0:128, :])
    for k in range(1, 8):
        acc = acc + dot(parts[32 * k : 32 * k + 32, :], final[128 * k : 128 * k + 128, :])
    for k in range(4):
        total[32 * k : 32 * k + 32, :] = acc[:, 128 * k : 128 * k + 128]
    for row in range(2):
        for k in range(2):
            re = total[pl.ds(32 * k + row, 16, stride=2), :]
            im = total[pl.ds(64 + 32 * k + row, 16, stride=2), :]
            pr = prop[row : row + 1, 128 * k : 128 * k + 128]
            pi = prop[row : row + 1, BAND + 128 * k : BAND + 128 * k + 128]
            cols = slice(row * BAND + 128 * k, row * BAND + 128 * k + 128)
            out[0, :, cols] = re * pr - im * pi
            out[1, :, cols] = re * pi + im * pr


VMEM = pl.BlockSpec(memory_space=pltpu.VMEM)
LIMIT = pltpu.CompilerParams(vmem_limit_bytes=12 * 1024 * 1024)
SMEM = pl.BlockSpec(memory_space=pltpu.SMEM)


def prepare(place, beams, right, back, chirp):
    return pl.pallas_call(
        prepare_kernel,
        in_specs=[SMEM] + [VMEM] * 5,
        out_specs=[VMEM] * 4,
        out_shape=[
            jax.ShapeDtypeStruct((G, 2 * G), F32),
            jax.ShapeDtypeStruct((4 * BLOCK, 2 * NQ), BF16),
            jax.ShapeDtypeStruct((NQ, 2 * NQ), F32),
            jax.ShapeDtypeStruct((2 * G, 2 * BAND), BF16),
        ],
        compiler_params=LIMIT,
        name="prepare",
    )(place, beams, right, back, chirp, chirp.T)


def main(cells, phi, right, left, back, inverse, prop):
    return pl.pallas_call(
        main_kernel,
        in_specs=[VMEM] * 7,
        out_specs=VMEM,
        out_shape=jax.ShapeDtypeStruct((BAND, 2 * BLOCK), BF16),
        scratch_shapes=[
            pltpu.VMEM((cells.shape[0], 128), F32),
            pltpu.VMEM((G, 2 * G), BF16),
            pltpu.VMEM((G, 2 * NQ), BF16),
            pltpu.VMEM((NQ, 2 * NQ), BF16),
            pltpu.VMEM((2 * NQ, 4 * BLOCK), BF16),
        ],
        compiler_params=LIMIT,
        name="propagate",
    )(cells, phi, right, left, back, inverse, prop)


def finish(parts, final, prop):
    return pl.pallas_call(
        final_kernel,
        in_specs=[VMEM] * 3,
        out_specs=VMEM,
        out_shape=jax.ShapeDtypeStruct((2, 16, 2 * BAND), F32),
        scratch_shapes=[pltpu.VMEM((128, 128), F32)],
        compiler_params=LIMIT,
        name="finish",
    )(parts, final, prop)


def own_coefficients(vectors, site):
    wave_x = vectors[:, 0]
    wave_y = vectors[:, 1]
    phases = jnp.mod(site[0] * wave_x + site[1] * wave_y, G)
    angle = -2.0 * math.pi / G * phases.astype(F32)
    weight = jnp.exp(-(wave_x * wave_x + wave_y * wave_y).astype(F32) * (8.0 / (BAND * BAND)))
    weight = weight * (1.0 / math.sqrt(vectors.shape[0]))
    coef_r = (weight * jnp.cos(angle)).astype(BF16).astype(F32) * G
    coef_i = (weight * jnp.sin(angle)).astype(BF16).astype(F32) * G
    offset = BAND // 2
    rows = [(wave_x + offset).astype(F32), (wave_y + offset).astype(F32), coef_r, coef_i]
    return jnp.concatenate([jnp.stack(rows, 0), jnp.zeros((4, vectors.shape[0]), F32)], 0)


def band_rows(first):
    fx = first + jnp.arange(2, dtype=jnp.int32) - BAND // 2
    fy = jnp.arange(BAND, dtype=jnp.int32) - BAND // 2
    squared = fx[:, None] * fx[:, None] + fy[None, :] * fy[None, :]
    inside = (9 * squared < G * G).astype(F32)
    angle = -2.0 * math.pi / (G * G) * jnp.mod(CHIRP_RATE * squared, G * G).astype(F32)
    return jnp.concatenate([inside * jnp.cos(angle), inside * jnp.sin(angle)], 1)


def message(potential, peers):
    near = potential[0].reshape(1, 8, 2, 128)
    far = potential[1].reshape(4, 8, BLOCK).swapaxes(0, 1).reshape(8, 1, 2, 128)
    far = jnp.broadcast_to(far, (8, peers // 8, 2, 128)).reshape(peers, 1, 2, 128)
    return jnp.concatenate([jnp.broadcast_to(near, (peers, 8, 2, 128)), far], 1)


def local(potential, wave_vectors, probe_sites):
    right, left, back, chirp = (jnp.asarray(t) for t in constant_tables())
    peers = lax.axis_size("beam")
    position = lax.axis_index("beam")
    probes = peers // 8
    cells = lax.all_to_all(message(potential, peers), "beam", 0, 0, tiled=True)
    site = lax.dynamic_index_in_dim(
        probe_sites, lax.axis_index("grp") * probes + position % probes, 0, keepdims=False
    )
    beams = own_coefficients(wave_vectors, site)
    place = (position // probes).reshape(1)
    phi, inverse, prop, final = prepare(place, beams, right, back, chirp)
    sent = main(cells.reshape(peers * ROWS, 128), phi, right, left, back, inverse, prop)
    parts = lax.all_to_all(sent.reshape(peers, 2, 128), "beam", 0, 0, tiled=True)
    return finish(parts.reshape(2 * peers, 128), final, band_rows(2 * position))


def solution(mesh):
    in_specs = (P(None, "beam"), P(), P())
    out_specs = P(None, "grp", "beam")
    return jax.shard_map(local, mesh=mesh, in_specs=in_specs, out_specs=out_specs, check_vma=False)
```

```python
import math

import jax
import jax.numpy as jnp
import numpy as np
from jax import lax
from jax.experimental import pallas as pl
from jax.experimental.pallas import tpu as pltpu
from jax.sharding import PartitionSpec as P

G = 512
BAND = 256
NQ = 384
PHASE_SCALE = 2.5
CHIRP_RATE = 20
BLOCK = 64
ROWS = 18

F32 = jnp.float32
BF16 = jnp.bfloat16


def frequencies():
    reach = math.isqrt((G * G - 1) // 9)
    band = np.arange(-BAND // 2, BAND // 2)
    high = np.arange(BAND // 2, reach + 1)
    low = np.arange(-reach, -BAND // 2)
    return np.concatenate([band, high, low])


def forward_table(places):
    freqs = frequencies()
    phases = np.mod(freqs[None, :] * places[:, None], G)
    angle = 2.0 * np.pi / G * phases
    table = np.zeros((2, places.shape[0], NQ), np.float64)
    table[0, :, : freqs.size] = np.cos(angle) / np.sqrt(G)
    table[1, :, : freqs.size] = -np.sin(angle) / np.sqrt(G)
    return table


def constant_tables():
    places = np.arange(G)
    permuted = (4 * np.arange(G // 4)[None, :] + np.arange(4)[:, None]).reshape(-1)
    natural = forward_table(places)
    shuffled = forward_table(permuted)
    right = np.concatenate([natural[0], natural[1]], 1)
    left = np.concatenate([shuffled[0].T, shuffled[1].T], 0)
    back = np.concatenate([shuffled[0], -shuffled[1]], 1)
    freqs = frequencies()
    squared = np.full((NQ,), 1.0e9)
    squared[: freqs.size] = freqs * freqs
    angle = np.zeros((NQ,))
    angle[: freqs.size] = -2.0 * np.pi / (G * G) * np.mod(CHIRP_RATE * freqs * freqs, G * G)
    chirp = np.stack([np.cos(angle), np.sin(angle), squared], 0)
    lanes = np.zeros((8, NQ))
    lanes[:3] = chirp
    return (
        right.astype(BF16),
        left.astype(BF16),
        back.astype(BF16),
        lanes.astype(np.float32),
    )


def half_turn_fits():
    nodes = 0.5 * np.cos(np.pi * (np.arange(400) + 0.5) / 400)
    square = nodes * nodes
    sine = np.polynomial.Polynomial.fit(square, np.sin(np.pi * nodes) / nodes, 4, domain=[0, 0.25])
    cosine = np.polynomial.Polynomial.fit(square, np.cos(np.pi * nodes), 4, domain=[0, 0.25])
    return (
        [float(v) for v in sine.convert().coef],
        [float(v) for v in cosine.convert().coef],
    )


SINE, COSINE = half_turn_fits()


def horner(coefs, x):
    total = coefs[-1]
    for coef in coefs[-2::-1]:
        total = total * x + coef
    return total


def phase_factor(cells):
    turns = cells * (PHASE_SCALE / (2.0 * math.pi))
    rest = turns - jnp.floor(turns + 0.5)
    square = rest * rest
    sine = rest * horner(SINE, square)
    cosine = horner(COSINE, square)
    return 1.0 - 2.0 * sine * sine, 2.0 * sine * cosine


def dot(a, b):
    return jnp.dot(a, b, preferred_element_type=F32)


def dot_t(a, b):
    return lax.dot_general(a, b, (((1,), (1,)), ((), ())), preferred_element_type=F32)


def prepare_kernel(place, beams, right, back, chirp, chirp_t, phi, inverse, prop):
    index = lax.broadcasted_iota(jnp.int32, (BAND, G), 0).astype(F32)
    on_x = index == beams[0:1, :]
    on_y = jnp.where(index == beams[1:2, :], 1.0, 0.0).astype(BF16)
    grid_r = dot_t(jnp.where(on_x, beams[2:3, :], 0.0).astype(BF16), on_y)
    grid_i = dot_t(jnp.where(on_x, beams[3:4, :], 0.0).astype(BF16), on_y)
    grid = jnp.concatenate([grid_r, grid_i], 1).astype(BF16)
    by_r = dot(back[:, 0:BAND], grid)
    by_i = dot(back[:, NQ : NQ + BAND], grid)
    mid_r = by_r[:, :BAND] - by_i[:, BAND:]
    mid_i = by_r[:, BAND:] + by_i[:, :BAND]
    band_r = right[:, 0:BAND]
    band_i = right[:, NQ : NQ + BAND]
    both = jnp.concatenate([band_r, band_i], 1)
    phi[:, :G] = dot_t(jnp.concatenate([mid_r, mid_i], 1).astype(BF16), both)
    phi[:, G:] = dot_t(jnp.concatenate([mid_i, -mid_r], 1).astype(BF16), both)
    start = pl.multiple_of(place[0] * BLOCK, BLOCK)
    own_r = right[pl.ds(start, BLOCK), 0:NQ]
    own_i = right[pl.ds(start, BLOCK), NQ:]
    inverse[0:64, :NQ] = own_r
    inverse[0:64, NQ:] = own_i
    inverse[64:128, :NQ] = -own_i
    inverse[64:128, NQ:] = own_r
    inverse[128:192, :NQ] = own_i
    inverse[128:192, NQ:] = -own_r
    inverse[192:256, :NQ] = own_r
    inverse[192:256, NQ:] = own_i
    inside = chirp_t[:, 2:3] + chirp[2:3, :] < (G * G - 1) // 9 + 0.5
    xr = chirp_t[:, 0:1]
    xi = chirp_t[:, 1:2]
    yr = chirp[0:1, :]
    yi = chirp[1:2, :]
    prop[:, :NQ] = jnp.where(inside, xr * yr - xi * yi, 0.0)
    prop[:, NQ:] = jnp.where(inside, xr * yi + xi * yr, 0.0)


def finish_table_kernel(right, sent, final):
    for k in range(G // BLOCK):
        rows = slice(k * BLOCK, (k + 1) * BLOCK)
        top = slice(2 * k * BLOCK, (2 * k + 1) * BLOCK)
        low = slice((2 * k + 1) * BLOCK, (2 * k + 2) * BLOCK)
        final[top, :BAND] = right[rows, 0:BAND]
        final[top, BAND:] = right[rows, NQ : NQ + BAND]
        final[low, :BAND] = -right[rows, NQ : NQ + BAND]
        final[low, BAND:] = right[rows, 0:BAND]


def main_kernel(
    cells, right, phi_far, left_far, inverse_far, prop_far, back_far, out,
    wide, data, half, spec, fold, phi, left, inverse, prop, back, phi_sems, sems,
):
    chunks = [
        pltpu.make_async_copy(
            phi_far.at[pl.ds(128 * j, 128), :], phi.at[pl.ds(128 * j, 128), :], phi_sems.at[j]
        )
        for j in range(4)
    ]
    for copy in chunks:
        copy.start()
    far = ((left_far, left), (prop_far, prop), (inverse_far, inverse), (back_far, back))
    copies = [pltpu.make_async_copy(a, b, sems.at[k]) for k, (a, b) in enumerate(far)]
    for copy in copies:
        copy.start()
    wide[...] = cells[...].astype(F32)
    for j in range(4):
        rows = slice(128 * j, 128 * j + 128)
        factors = [
            phase_factor(wide[pl.ds(4 * j + h, 128, stride=ROWS), :]) for h in range(4)
        ]
        chunks[j].wait()
        for h in range(4):
            cols = slice(128 * h, 128 * h + 128)
            cos, sin = factors[h]
            pr = phi[rows, 128 * h : 128 * h + 128]
            pi = phi[rows, G + 128 * h : G + 128 * h + 128]
            data[rows, cols] = (pr * cos - pi * sin).astype(BF16)
            data[rows, G + 128 * h : G + 128 * h + 128] = (pr * sin + pi * cos).astype(BF16)
        one = dot(data[rows, :G], right[...])
        two = dot(data[rows, G:], right[...])
        half[rows, :NQ] = (one[:, :NQ] - two[:, NQ:]).astype(BF16)
        half[rows, NQ:] = (one[:, NQ:] + two[:, :NQ]).astype(BF16)
    for copy in copies:
        copy.wait()
    for j in range(3):
        rows = slice(128 * j, 128 * j + 128)
        one = dot(left[rows, :], half[...])
        two = dot(left[NQ + 128 * j : NQ + 128 * j + 128, :], half[...])
        re = one[:, :NQ] - two[:, NQ:]
        im = one[:, NQ:] + two[:, :NQ]
        pr = prop[rows, :NQ]
        pi = prop[rows, NQ:]
        spec[rows, :NQ] = (re * pr - im * pi).astype(BF16)
        spec[rows, NQ:] = (re * pi + im * pr).astype(BF16)
        turned = dot_t(spec[rows, :], inverse[...])
        low = slice(NQ + 128 * j, NQ + 128 * j + 128)
        fold[rows, :] = turned.astype(BF16)
        fold[low, :128] = turned[:, 128:].astype(BF16)
        fold[low, 128:] = (-turned[:, :128]).astype(BF16)
    lane = lax.broadcasted_iota(jnp.int32, (128, 128), 1) < BLOCK
    for j in range(4):
        rows = slice(128 * j, 128 * j + 128)
        pair = wide[pl.ds(16 + j // 2, 128, stride=ROWS), :]
        other = pltpu.roll(pair, BLOCK, 1)
        own = jnp.where(lane, pair, other) if j % 2 == 0 else jnp.where(lane, other, pair)
        cos, sin = phase_factor(own)
        wave = dot(back[rows, :], fold[...])
        data[rows, :128] = (wave[:, :128] * cos + wave[:, 128:] * sin).astype(BF16)
        data[rows, 128:256] = (wave[:, 128:] * cos - wave[:, :128] * sin).astype(BF16)
    total = dot(left[0:BAND, :], data[:, :128]) + dot(left[NQ : NQ + BAND, :], data[:, 128:256])
    out[...] = total.astype(BF16)


def final_kernel(parts, final, prop, out, total):
    acc = dot(parts[0:32, :], final[0:128, :])
    for k in range(1, 8):
        acc = acc + dot(parts[32 * k : 32 * k + 32, :], final[128 * k : 128 * k + 128, :])
    for k in range(4):
        total[32 * k : 32 * k + 32, :] = acc[:, 128 * k : 128 * k + 128]
    for row in range(2):
        for k in range(2):
            re = total[pl.ds(32 * k + row, 16, stride=2), :]
            im = total[pl.ds(64 + 32 * k + row, 16, stride=2), :]
            pr = prop[row : row + 1, 128 * k : 128 * k + 128]
            pi = prop[row : row + 1, BAND + 128 * k : BAND + 128 * k + 128]
            cols = slice(row * BAND + 128 * k, row * BAND + 128 * k + 128)
            out[0, :, cols] = re * pr - im * pi
            out[1, :, cols] = re * pi + im * pr


VMEM = pl.BlockSpec(memory_space=pltpu.VMEM)
LIMIT = pltpu.CompilerParams(vmem_limit_bytes=16 * 1024 * 1024)
FAR = pl.BlockSpec(memory_space=pltpu.HBM)
SMEM = pl.BlockSpec(memory_space=pltpu.SMEM)


def prepare(place, beams, right, back, chirp):
    return pl.pallas_call(
        prepare_kernel,
        in_specs=[SMEM] + [VMEM] * 5,
        out_specs=[VMEM] * 3,
        out_shape=[
            pltpu.HBM((G, 2 * G), F32),
            pltpu.HBM((4 * BLOCK, 2 * NQ), BF16),
            pltpu.HBM((NQ, 2 * NQ), F32),
        ],
        compiler_params=LIMIT,
        name="prepare",
    )(place, beams, right, back, chirp, chirp.T)


def main(cells, right, phi, left, inverse, prop, back):
    return pl.pallas_call(
        main_kernel,
        in_specs=[VMEM] * 2 + [FAR] * 5,
        out_specs=VMEM,
        out_shape=jax.ShapeDtypeStruct((BAND, 2 * BLOCK), BF16),
        scratch_shapes=[
            pltpu.VMEM((cells.shape[0], 128), F32),
            pltpu.VMEM((G, 2 * G), BF16),
            pltpu.VMEM((G, 2 * NQ), BF16),
            pltpu.VMEM((NQ, 2 * NQ), BF16),
            pltpu.VMEM((2 * NQ, 4 * BLOCK), BF16),
            pltpu.VMEM(phi.shape, F32),
            pltpu.VMEM(left.shape, BF16),
            pltpu.VMEM(inverse.shape, BF16),
            pltpu.VMEM(prop.shape, F32),
            pltpu.VMEM(back.shape, BF16),
            pltpu.SemaphoreType.DMA((4,)),
            pltpu.SemaphoreType.DMA((4,)),
        ],
        compiler_params=LIMIT,
        name="propagate",
    )(cells, right, phi, left, inverse, prop, back)


placed = pltpu.with_memory_space_constraint


def finish_table(right, sent):
    return pl.pallas_call(
        finish_table_kernel,
        in_specs=[VMEM, FAR],
        out_specs=VMEM,
        out_shape=jax.ShapeDtypeStruct((2 * G, 2 * BAND), BF16),
        compiler_params=LIMIT,
        name="finish_table",
    )(right, sent)


def finish(parts, final, prop):
    return pl.pallas_call(
        final_kernel,
        in_specs=[VMEM] * 3,
        out_specs=VMEM,
        out_shape=jax.ShapeDtypeStruct((2, 16, 2 * BAND), F32),
        scratch_shapes=[pltpu.VMEM((128, 128), F32)],
        compiler_params=LIMIT,
        name="finish",
    )(parts, final, prop)


def own_coefficients(vectors, site):
    wave_x = vectors[:, 0]
    wave_y = vectors[:, 1]
    phases = jnp.mod(site[0] * wave_x + site[1] * wave_y, G)
    angle = -2.0 * math.pi / G * phases.astype(F32)
    weight = jnp.exp(-(wave_x * wave_x + wave_y * wave_y).astype(F32) * (8.0 / (BAND * BAND)))
    weight = weight * (1.0 / math.sqrt(vectors.shape[0]))
    coef_r = (weight * jnp.cos(angle)).astype(BF16).astype(F32) * G
    coef_i = (weight * jnp.sin(angle)).astype(BF16).astype(F32) * G
    offset = BAND // 2
    rows = [(wave_x + offset).astype(F32), (wave_y + offset).astype(F32), coef_r, coef_i]
    return jnp.concatenate([jnp.stack(rows, 0), jnp.zeros((4, vectors.shape[0]), F32)], 0)


def band_rows(first):
    fx = first + jnp.arange(2, dtype=jnp.int32) - BAND // 2
    fy = jnp.arange(BAND, dtype=jnp.int32) - BAND // 2
    squared = fx[:, None] * fx[:, None] + fy[None, :] * fy[None, :]
    inside = (9 * squared < G * G).astype(F32)
    angle = -2.0 * math.pi / (G * G) * jnp.mod(CHIRP_RATE * squared, G * G).astype(F32)
    return jnp.concatenate([inside * jnp.cos(angle), inside * jnp.sin(angle)], 1)


def message_kernel(cells, out, rows, block):
    wide = cells[...].astype(F32)
    for k in range(16):
        rows[k : k + 1, :] = wide[0:1, 128 * k : 128 * k + 128]
    near = rows[...]
    for m in range(8):
        block[ROWS * m : ROWS * m + 16, :] = near
    low = lax.broadcasted_iota(jnp.int32, (1, 128), 1) < BLOCK
    for r in range(8):
        for h in range(2):
            at = 128 * (8 * h + r // 2)
            one = wide[1:2, at : at + 128]
            two = wide[1:2, at + G : at + G + 128]
            if r % 2 == 0:
                own = jnp.where(low, one, pltpu.roll(two, BLOCK, 1))
            else:
                own = jnp.where(low, pltpu.roll(one, BLOCK, 1), two)
            for m in range(8):
                block[ROWS * m + 16 + h : ROWS * m + 17 + h, :] = own
        copies = block[...].astype(BF16)
        size = 8 * ROWS
        out[2 * r * size : (2 * r + 1) * size, :] = copies
        out[(2 * r + 1) * size : (2 * r + 2) * size, :] = copies


def message(potential):
    return pl.pallas_call(
        message_kernel,
        in_specs=[VMEM],
        out_specs=VMEM,
        out_shape=pltpu.VMEM((128 * ROWS, 128), BF16),
        scratch_shapes=[pltpu.VMEM((16, 128), F32), pltpu.VMEM((8 * ROWS, 128), F32)],
        compiler_params=LIMIT,
        name="message",
    )(potential)


def local(potential, wave_vectors, probe_sites):
    right, left, back, chirp = (jnp.asarray(t) for t in constant_tables())
    peers = lax.axis_size("beam")
    position = lax.axis_index("beam")
    probes = peers // 8
    mine = message(potential).reshape(peers, ROWS // 2, 2, 128)
    cells = lax.all_to_all(mine, "beam", 0, 0, tiled=True)
    site = lax.dynamic_index_in_dim(
        probe_sites, lax.axis_index("grp") * probes + position % probes, 0, keepdims=False
    )
    beams = own_coefficients(wave_vectors, site)
    place = (position // probes).reshape(1)
    phi, inverse, prop = prepare(place, beams, right, back, chirp)
    near = [placed(a, pltpu.VMEM) for a in (cells.reshape(peers * ROWS, 128), right)]
    far = [placed(a, pltpu.HBM) for a in (phi, left, inverse, prop, back)]
    sent = main(*near, *far)
    parts = lax.all_to_all(sent.reshape(peers, 2, 128), "beam", 0, 0, tiled=True)
    final = finish_table(right, sent)
    return finish(parts.reshape(2 * peers, 128), final, band_rows(2 * position))


def solution(mesh):
    in_specs = (P(None, "beam"), P(), P())
    out_specs = P(None, "grp", "beam")
    return jax.shard_map(local, mesh=mesh, in_specs=in_specs, out_specs=out_specs, check_vma=False)
```

```python
import math

import jax
import jax.numpy as jnp
import numpy as np
from jax import lax
from jax.experimental import pallas as pl
from jax.experimental.pallas import tpu as pltpu
from jax.sharding import PartitionSpec as P

G = 512
BAND = 256
NQ = 384
PHASE_SCALE = 2.5
CHIRP_RATE = 20
BLOCK = 64
ROWS = 10

F32 = jnp.float32
BF16 = jnp.bfloat16


def frequencies():
    reach = math.isqrt((G * G - 1) // 9)
    band = np.arange(-BAND // 2, BAND // 2)
    high = np.arange(BAND // 2, reach + 1)
    low = np.arange(-reach, -BAND // 2)
    return np.concatenate([band, high, low])


def forward_table(places):
    freqs = frequencies()
    phases = np.mod(freqs[None, :] * places[:, None], G)
    angle = 2.0 * np.pi / G * phases
    table = np.zeros((2, places.shape[0], NQ), np.float64)
    table[0, :, : freqs.size] = np.cos(angle) / np.sqrt(G)
    table[1, :, : freqs.size] = -np.sin(angle) / np.sqrt(G)
    return table


def constant_tables():
    places = np.arange(G)
    permuted = (4 * np.arange(G // 4)[None, :] + np.arange(4)[:, None]).reshape(-1)
    natural = forward_table(places)
    shuffled = forward_table(permuted)
    right = np.concatenate([natural[0], natural[1]], 1)
    left = np.concatenate([shuffled[0].T, shuffled[1].T], 0)
    back = np.concatenate([shuffled[0], -shuffled[1]], 1)
    freqs = frequencies()
    squared = np.full((NQ,), 1.0e9)
    squared[: freqs.size] = freqs * freqs
    angle = np.zeros((NQ,))
    angle[: freqs.size] = -2.0 * np.pi / (G * G) * np.mod(CHIRP_RATE * freqs * freqs, G * G)
    chirp = np.stack([np.cos(angle), np.sin(angle), squared], 0)
    lanes = np.zeros((8, NQ))
    lanes[:3] = chirp
    return (
        right.astype(BF16),
        left.astype(BF16),
        back.astype(BF16),
        lanes.astype(np.float32),
    )


def half_turn_fits():
    nodes = 0.5 * np.cos(np.pi * (np.arange(400) + 0.5) / 400)
    square = nodes * nodes
    sine = np.polynomial.Polynomial.fit(square, np.sin(np.pi * nodes) / nodes, 4, domain=[0, 0.25])
    cosine = np.polynomial.Polynomial.fit(square, np.cos(np.pi * nodes), 4, domain=[0, 0.25])
    return (
        [float(v) for v in sine.convert().coef],
        [float(v) for v in cosine.convert().coef],
    )


SINE, COSINE = half_turn_fits()


def horner(coefs, x):
    total = coefs[-1]
    for coef in coefs[-2::-1]:
        total = total * x + coef
    return total


def phase_factor(cells):
    turns = cells * (PHASE_SCALE / (2.0 * math.pi))
    rest = turns - jnp.floor(turns + 0.5)
    square = rest * rest
    sine = rest * horner(SINE, square)
    cosine = horner(COSINE, square)
    return 1.0 - 2.0 * sine * sine, 2.0 * sine * cosine


def own_core():
    return lax.axis_index("grp") % 2


def dot(a, b):
    return jnp.dot(a, b, preferred_element_type=F32)


def dot_t(a, b):
    return lax.dot_general(a, b, (((1,), (1,)), ((), ())), preferred_element_type=F32)


def prepare_kernel(beams, right, back, chirp, chirp_t, phi, inverse, prop):
    index = lax.broadcasted_iota(jnp.int32, (BAND, G), 0).astype(F32)
    on_x = index == beams[0:1, :]
    on_y = jnp.where(index == beams[1:2, :], 1.0, 0.0).astype(BF16)
    grid_r = dot_t(jnp.where(on_x, beams[2:3, :], 0.0).astype(BF16), on_y)
    grid_i = dot_t(jnp.where(on_x, beams[3:4, :], 0.0).astype(BF16), on_y)
    grid = jnp.concatenate([grid_r, grid_i], 1).astype(BF16)
    by_r = dot(back[:, 0:BAND], grid)
    by_i = dot(back[:, NQ : NQ + BAND], grid)
    mid_r = by_r[:, :BAND] - by_i[:, BAND:]
    mid_i = by_r[:, BAND:] + by_i[:, :BAND]
    band_r = right[:, 0:BAND]
    band_i = right[:, NQ : NQ + BAND]
    both = jnp.concatenate([band_r, band_i], 1)
    phi[:, :G] = dot_t(jnp.concatenate([mid_r, mid_i], 1).astype(BF16), both).astype(BF16)
    phi[:, G:] = dot_t(jnp.concatenate([mid_i, -mid_r], 1).astype(BF16), both).astype(BF16)
    start = pl.multiple_of(lax.axis_index("beam") // 16 * BLOCK, BLOCK)
    own_r = right[pl.ds(start, BLOCK), 0:NQ]
    own_i = right[pl.ds(start, BLOCK), NQ:]
    inverse[0:64, :NQ] = own_r
    inverse[0:64, NQ:] = own_i
    inverse[64:128, :NQ] = -own_i
    inverse[64:128, NQ:] = own_r
    inverse[128:192, :NQ] = own_i
    inverse[128:192, NQ:] = -own_r
    inverse[192:256, :NQ] = own_r
    inverse[192:256, NQ:] = own_i
    inside = chirp_t[:, 2:3] + chirp[2:3, :] < (G * G - 1) // 9 + 0.5
    xr = chirp_t[:, 0:1]
    xi = chirp_t[:, 1:2]
    yr = chirp[0:1, :]
    yi = chirp[1:2, :]
    prop[:, :NQ] = jnp.where(inside, xr * yr - xi * yi, 0.0)
    prop[:, NQ:] = jnp.where(inside, xr * yi + xi * yr, 0.0)


def finish_table_kernel(right, sent, final):
    for k in range(G // BLOCK):
        rows = slice(k * BLOCK, (k + 1) * BLOCK)
        top = slice(2 * k * BLOCK, (2 * k + 1) * BLOCK)
        low = slice((2 * k + 1) * BLOCK, (2 * k + 2) * BLOCK)
        final[top, :BAND] = right[rows, 0:BAND]
        final[top, BAND:] = right[rows, NQ : NQ + BAND]
        final[low, :BAND] = -right[rows, NQ : NQ + BAND]
        final[low, BAND:] = right[rows, 0:BAND]


def forward_rows(wide, phi, right, data, half, first, offset):
    for j in range(2):
        rows = slice(128 * j, 128 * j + 128)
        probe = pl.ds(pl.multiple_of(first + 128 * j, 128), 128)
        for h in range(4):
            cos, sin = phase_factor(wide[pl.ds(4 * j + h, 128, stride=ROWS), :])
            pr = phi[probe, 128 * h : 128 * h + 128].astype(F32)
            pi = phi[probe, G + 128 * h : G + 128 * h + 128].astype(F32)
            data[rows, 128 * h : 128 * h + 128] = (pr * cos - pi * sin).astype(BF16)
            data[rows, G + 128 * h : G + 128 * h + 128] = (pr * sin + pi * cos).astype(BF16)
        one = dot(data[rows, :G], right[...])
        two = dot(data[rows, G:], right[...])
        kept = pl.ds(pl.multiple_of(offset + 128 * j, 128), 128)
        half[kept, :NQ] = (one[:, :NQ] - two[:, NQ:]).astype(BF16)
        half[kept, NQ:] = (one[:, NQ:] + two[:, :NQ]).astype(BF16)


def early_kernel(cells, phi, right, half, wide, data):
    wide[...] = cells[...].astype(F32)
    forward_rows(wide, phi, right, data, half, own_core() * 256, 0)


def main_kernel(
    other, cells, early, right, phi, left_far, inverse_far, prop_far, back_far, out,
    wide, data, half, spec, fold, last, left, inverse, prop, back, sems,
):
    far = ((left_far, left), (prop_far, prop), (inverse_far, inverse), (back_far, back))
    copies = [pltpu.make_async_copy(a, b, sems.at[k]) for k, (a, b) in enumerate(far)]
    for copy in copies:
        copy.start()
    wide[...] = other[...].astype(F32)
    start = own_core() * 256
    half[pl.ds(pl.multiple_of(start, 256), 256), :] = early[...]
    forward_rows(wide, phi, right, data, half, 256 - start, 256 - start)
    wide[...] = cells[...].astype(F32)
    for copy in copies[:3]:
        copy.wait()
    for j in range(3):
        rows = slice(128 * j, 128 * j + 128)
        one = dot(left[rows, :], half[...])
        two = dot(left[NQ + 128 * j : NQ + 128 * j + 128, :], half[...])
        re = one[:, :NQ] - two[:, NQ:]
        im = one[:, NQ:] + two[:, :NQ]
        pr = prop[rows, :NQ]
        pi = prop[rows, NQ:]
        spec[rows, :NQ] = (re * pr - im * pi).astype(BF16)
        spec[rows, NQ:] = (re * pi + im * pr).astype(BF16)
        turned = dot_t(spec[rows, :], inverse[...])
        low = slice(NQ + 128 * j, NQ + 128 * j + 128)
        fold[rows, :] = turned.astype(BF16)
        fold[low, :128] = turned[:, 128:].astype(BF16)
        fold[low, 128:] = (-turned[:, :128]).astype(BF16)
    lane = lax.broadcasted_iota(jnp.int32, (128, 128), 1) < BLOCK
    copies[3].wait()
    for j in range(4):
        rows = slice(128 * j, 128 * j + 128)
        pair = wide[pl.ds(8 + j // 2, 128, stride=ROWS), :]
        swapped = pltpu.roll(pair, BLOCK, 1)
        own = jnp.where(lane, pair, swapped) if j % 2 == 0 else jnp.where(lane, swapped, pair)
        cos, sin = phase_factor(own)
        wave = dot(back[rows, :], fold[...])
        last[rows, :128] = (wave[:, :128] * cos + wave[:, 128:] * sin).astype(BF16)
        last[rows, 128:] = (wave[:, 128:] * cos - wave[:, :128] * sin).astype(BF16)
    total = dot(left[0:BAND, :], last[:, :128]) + dot(left[NQ : NQ + BAND, :], last[:, 128:])
    out[...] = total.astype(BF16)


def final_kernel(parts, final, prop, out, total):
    acc = dot(parts[0:32, :], final[0:128, :])
    for k in range(1, 8):
        acc = acc + dot(parts[32 * k : 32 * k + 32, :], final[128 * k : 128 * k + 128, :])
    for k in range(4):
        total[32 * k : 32 * k + 32, :] = acc[:, 128 * k : 128 * k + 128]
    for row in range(2):
        for k in range(2):
            re = total[pl.ds(32 * k + row, 16, stride=2), :]
            im = total[pl.ds(64 + 32 * k + row, 16, stride=2), :]
            pr = prop[row : row + 1, 128 * k : 128 * k + 128]
            pi = prop[row : row + 1, BAND + 128 * k : BAND + 128 * k + 128]
            cols = slice(row * BAND + 128 * k, row * BAND + 128 * k + 128)
            out[0, :, cols] = re * pr - im * pi
            out[1, :, cols] = re * pi + im * pr


VMEM = pl.BlockSpec(memory_space=pltpu.VMEM)
LIMIT = pltpu.CompilerParams(vmem_limit_bytes=16 * 1024 * 1024)
FAR = pl.BlockSpec(memory_space=pltpu.HBM)


def prepare(beams, right, back, chirp):
    return pl.pallas_call(
        prepare_kernel,
        in_specs=[VMEM] * 5,
        out_specs=[VMEM] * 3,
        out_shape=[
            pltpu.VMEM((G, 2 * G), BF16),
            pltpu.HBM((4 * BLOCK, 2 * NQ), BF16),
            pltpu.HBM((NQ, 2 * NQ), F32),
        ],
        compiler_params=LIMIT,
        name="prepare",
    )(beams, right, back, chirp, chirp.T)


def early(cells, phi, right):
    return pl.pallas_call(
        early_kernel,
        in_specs=[VMEM] * 3,
        out_specs=VMEM,
        out_shape=pltpu.VMEM((G // 2, 2 * NQ), BF16),
        scratch_shapes=[
            pltpu.VMEM((cells.shape[0], 128), F32),
            pltpu.VMEM((G // 2, 2 * G), BF16),
        ],
        compiler_params=LIMIT,
        name="early",
    )(cells, phi, right)


def main(near, far):
    rows = near[0].shape[0]
    return pl.pallas_call(
        main_kernel,
        in_specs=[VMEM] * 5 + [FAR] * 4,
        out_specs=VMEM,
        out_shape=jax.ShapeDtypeStruct((BAND, 2 * BLOCK), BF16),
        scratch_shapes=[
            pltpu.VMEM((rows, 128), F32),
            pltpu.VMEM((G // 2, 2 * G), BF16),
            pltpu.VMEM((G, 2 * NQ), BF16),
            pltpu.VMEM((NQ, 2 * NQ), BF16),
            pltpu.VMEM((2 * NQ, 4 * BLOCK), BF16),
            pltpu.VMEM((G, 4 * BLOCK), BF16),
        ]
        + [pltpu.VMEM(a.shape, a.dtype) for a in far]
        + [pltpu.SemaphoreType.DMA((4,))],
        compiler_params=LIMIT,
        name="propagate",
    )(*near, *far)


def finish_table(right, sent):
    return pl.pallas_call(
        finish_table_kernel,
        in_specs=[VMEM, FAR],
        out_specs=VMEM,
        out_shape=jax.ShapeDtypeStruct((2 * G, 2 * BAND), BF16),
        compiler_params=LIMIT,
        name="finish_table",
    )(right, sent)


placed = pltpu.with_memory_space_constraint


def finish(parts, final, prop):
    return pl.pallas_call(
        final_kernel,
        in_specs=[VMEM] * 3,
        out_specs=VMEM,
        out_shape=jax.ShapeDtypeStruct((2, 16, 2 * BAND), F32),
        scratch_shapes=[pltpu.VMEM((128, 128), F32)],
        compiler_params=LIMIT,
        name="finish",
    )(parts, final, prop)


def own_coefficients(vectors, site):
    wave_x = vectors[:, 0]
    wave_y = vectors[:, 1]
    phases = jnp.mod(site[0] * wave_x + site[1] * wave_y, G)
    angle = -2.0 * math.pi / G * phases.astype(F32)
    weight = jnp.exp(-(wave_x * wave_x + wave_y * wave_y).astype(F32) * (8.0 / (BAND * BAND)))
    weight = weight * (1.0 / math.sqrt(vectors.shape[0]))
    coef_r = (weight * jnp.cos(angle)).astype(BF16).astype(F32) * G
    coef_i = (weight * jnp.sin(angle)).astype(BF16).astype(F32) * G
    offset = BAND // 2
    rows = [(wave_x + offset).astype(F32), (wave_y + offset).astype(F32), coef_r, coef_i]
    return jnp.concatenate([jnp.stack(rows, 0), jnp.zeros((4, vectors.shape[0]), F32)], 0)


def band_rows(first):
    fx = first + jnp.arange(2, dtype=jnp.int32) - BAND // 2
    fy = jnp.arange(BAND, dtype=jnp.int32) - BAND // 2
    squared = fx[:, None] * fx[:, None] + fy[None, :] * fy[None, :]
    inside = (9 * squared < G * G).astype(F32)
    angle = -2.0 * math.pi / (G * G) * jnp.mod(CHIRP_RATE * squared, G * G).astype(F32)
    return jnp.concatenate([inside * jnp.cos(angle), inside * jnp.sin(angle)], 1)


def message_kernel(cells, out, rows, block):
    wide = cells[...].astype(F32)
    near = jnp.where(own_core() == 0, wide[0:1, : 2 * G], wide[0:1, 2 * G :])
    for k in range(8):
        rows[k : k + 1, :] = near[:, 128 * k : 128 * k + 128]
    near = rows[...]
    for m in range(8):
        block[ROWS * m : ROWS * m + 8, :] = near
    low = lax.broadcasted_iota(jnp.int32, (1, 128), 1) < BLOCK
    for r in range(8):
        for h in range(2):
            at = 128 * (8 * h + r // 2)
            one = wide[1:2, at : at + 128]
            two = wide[1:2, at + G : at + G + 128]
            if r % 2 == 0:
                own = jnp.where(low, one, pltpu.roll(two, BLOCK, 1))
            else:
                own = jnp.where(low, pltpu.roll(one, BLOCK, 1), two)
            for m in range(8):
                block[ROWS * m + 8 + h : ROWS * m + 9 + h, :] = own
        copies = block[...].astype(BF16)
        size = 8 * ROWS
        out[2 * r * size : (2 * r + 1) * size, :] = copies
        out[(2 * r + 1) * size : (2 * r + 2) * size, :] = copies


def message(potential):
    return pl.pallas_call(
        message_kernel,
        in_specs=[VMEM],
        out_specs=VMEM,
        out_shape=jax.ShapeDtypeStruct((128 * ROWS, 128), BF16),
        scratch_shapes=[pltpu.VMEM((8, 128), F32), pltpu.VMEM((8 * ROWS, 128), F32)],
        compiler_params=LIMIT,
        name="message",
    )(potential)


def near_groups(peers):
    groups = []
    for turn in range(2):
        for core in range(2):
            groups.append([4 * k + 2 * ((k + turn) % 2) + core for k in range(peers)])
    return groups


def local(potential, wave_vectors, probe_sites):
    right, left, back, chirp = (jnp.asarray(t) for t in constant_tables())
    peers = lax.axis_size("beam")
    position = lax.axis_index("beam")
    probes = peers // 8
    group = lax.axis_index("grp")
    mine = message(potential).reshape(peers, ROWS // 2, 2, 128)
    cells = lax.all_to_all(
        mine, ("beam", "grp"), 0, 0, tiled=True, axis_index_groups=near_groups(peers)
    )
    site = lax.dynamic_index_in_dim(
        probe_sites, group * probes + position % probes, 0, keepdims=False
    )
    beams = own_coefficients(wave_vectors, site)
    made = prepare(beams, right, back, chirp)
    cells, phi, inverse, prop = lax.optimization_barrier((cells, *made))
    cells = cells.reshape(peers * ROWS, 128)
    other = lax.ppermute(cells, "grp", [(0, 1), (1, 0), (2, 3), (3, 2)])
    cells, right_near, phi = (placed(a, pltpu.VMEM) for a in (cells, right, phi))
    first = placed(early(cells, phi, right_near), pltpu.VMEM)
    near = (placed(other, pltpu.VMEM), cells, first, right_near, phi)
    far = [placed(a, pltpu.HBM) for a in (left, inverse, prop, back)]
    sent = main(near, far)
    parts = lax.all_to_all(sent.reshape(peers, 2, 128), "beam", 0, 0, tiled=True)
    final = finish_table(right, sent)
    return finish(parts.reshape(2 * peers, 128), final, band_rows(2 * position))


def solution(mesh):
    in_specs = (P(None, "beam"), P(), P())
    out_specs = P(None, "grp", "beam")
    return jax.shard_map(local, mesh=mesh, in_specs=in_specs, out_specs=out_specs, check_vma=False)
```

```python
import math

import jax
import jax.numpy as jnp
import numpy as np
from jax import lax
from jax.experimental import pallas as pl
from jax.experimental.pallas import tpu as pltpu
from jax.sharding import PartitionSpec as P

G = 512
BAND = 256
NQ = 384
PHASE_SCALE = 2.5
CHIRP_RATE = 20
PEERS = 32
HALF = 256
ROWS = 12

F32 = jnp.float32
BF16 = jnp.bfloat16


def frequencies():
    reach = math.isqrt((G * G - 1) // 9)
    band = np.arange(-BAND // 2, BAND // 2)
    high = np.arange(BAND // 2, reach + 1)
    low = np.arange(-reach, -BAND // 2)
    return np.concatenate([band, high, low])


def forward_table(places):
    freqs = frequencies()
    phases = np.mod(freqs[None, :] * places[:, None], G)
    angle = 2.0 * np.pi / G * phases
    table = np.zeros((2, places.shape[0], NQ), np.float64)
    table[0, :, : freqs.size] = np.cos(angle) / np.sqrt(G)
    table[1, :, : freqs.size] = -np.sin(angle) / np.sqrt(G)
    return table


def constant_tables():
    places = np.arange(G)
    permuted = (4 * np.arange(G // 4)[None, :] + np.arange(4)[:, None]).reshape(-1)
    natural = forward_table(places)
    shuffled = forward_table(permuted)
    right = np.concatenate([natural[0], natural[1]], 1)
    left = np.concatenate([shuffled[0].T, shuffled[1].T], 0)
    back = np.concatenate([shuffled[0], -shuffled[1]], 1)
    freqs = frequencies()
    squared = np.full((NQ,), 1.0e9)
    squared[: freqs.size] = freqs * freqs
    angle = np.zeros((NQ,))
    angle[: freqs.size] = -2.0 * np.pi / (G * G) * np.mod(CHIRP_RATE * freqs * freqs, G * G)
    chirp = np.stack([np.cos(angle), np.sin(angle), squared], 0)
    lanes = np.zeros((8, NQ))
    lanes[:3] = chirp
    return (
        right.astype(BF16),
        left.astype(BF16),
        back.astype(BF16),
        lanes.astype(np.float32),
    )


def half_turn_fits():
    nodes = 0.5 * np.cos(np.pi * (np.arange(400) + 0.5) / 400)
    square = nodes * nodes
    sine = np.polynomial.Polynomial.fit(square, np.sin(np.pi * nodes) / nodes, 4, domain=[0, 0.25])
    cosine = np.polynomial.Polynomial.fit(square, np.cos(np.pi * nodes), 4, domain=[0, 0.25])
    return (
        [float(v) for v in sine.convert().coef],
        [float(v) for v in cosine.convert().coef],
    )


SINE, COSINE = half_turn_fits()


def horner(coefs, x):
    total = coefs[-1]
    for coef in coefs[-2::-1]:
        total = total * x + coef
    return total


def phase_factor(cells):
    turns = cells * (PHASE_SCALE / (2.0 * math.pi))
    rest = turns - jnp.floor(turns + 0.5)
    square = rest * rest
    sine = rest * horner(SINE, square)
    cosine = horner(COSINE, square)
    return 1.0 - 2.0 * sine * sine, 2.0 * sine * cosine


def own_core():
    return lax.axis_index("grp") % 2


def dot(a, b):
    return jnp.dot(a, b, preferred_element_type=F32)


def dot_t(a, b):
    return lax.dot_general(a, b, (((1,), (1,)), ((), ())), preferred_element_type=F32)


def prepare_kernel(beams, right, back, chirp, chirp_t, phi, prop):
    index = lax.broadcasted_iota(jnp.int32, (BAND, G), 0).astype(F32)
    on_x = index == beams[0:1, :]
    on_y = jnp.where(index == beams[1:2, :], 1.0, 0.0).astype(BF16)
    grid_r = dot_t(jnp.where(on_x, beams[2:3, :], 0.0).astype(BF16), on_y)
    grid_i = dot_t(jnp.where(on_x, beams[3:4, :], 0.0).astype(BF16), on_y)
    grid = jnp.concatenate([grid_r, grid_i], 1).astype(BF16)
    by_r = dot(back[:, 0:BAND], grid)
    by_i = dot(back[:, NQ : NQ + BAND], grid)
    mid_r = by_r[:, :BAND] - by_i[:, BAND:]
    mid_i = by_r[:, BAND:] + by_i[:, :BAND]
    band_r = right[:, 0:BAND]
    band_i = right[:, NQ : NQ + BAND]
    both = jnp.concatenate([band_r, band_i], 1)
    phi[:, :G] = dot_t(jnp.concatenate([mid_r, mid_i], 1).astype(BF16), both).astype(BF16)
    phi[:, G:] = dot_t(jnp.concatenate([mid_i, -mid_r], 1).astype(BF16), both).astype(BF16)
    inside = chirp_t[:, 2:3] + chirp[2:3, :] < (G * G - 1) // 9 + 0.5
    xr = chirp_t[:, 0:1]
    xi = chirp_t[:, 1:2]
    yr = chirp[0:1, :]
    yi = chirp[1:2, :]
    prop[:, :NQ] = jnp.where(inside, xr * yr - xi * yi, 0.0)
    prop[:, NQ:] = jnp.where(inside, xr * yi + xi * yr, 0.0)


def finish_table_kernel(right, sent, final):
    for h in range(2):
        rows = slice(h * HALF, h * HALF + HALF)
        top = slice(2 * h * HALF, (2 * h + 1) * HALF)
        low = slice((2 * h + 1) * HALF, (2 * h + 2) * HALF)
        final[top, :BAND] = right[rows, 0:BAND]
        final[top, BAND:] = right[rows, NQ : NQ + BAND]
        final[low, :BAND] = -right[rows, NQ : NQ + BAND]
        final[low, BAND:] = right[rows, 0:BAND]


def forward_rows(wide, phi, right, data, half, first, offset):
    for j in range(2):
        rows = slice(128 * j, 128 * j + 128)
        probe = pl.ds(pl.multiple_of(first + 128 * j, 128), 128)
        for h in range(4):
            cos, sin = phase_factor(wide[pl.ds(4 * j + h, 128, stride=ROWS), :])
            pr = phi[probe, 128 * h : 128 * h + 128].astype(F32)
            pi = phi[probe, G + 128 * h : G + 128 * h + 128].astype(F32)
            data[rows, 128 * h : 128 * h + 128] = (pr * cos - pi * sin).astype(BF16)
            data[rows, G + 128 * h : G + 128 * h + 128] = (pr * sin + pi * cos).astype(BF16)
        one = dot(data[rows, :G], right[...])
        two = dot(data[rows, G:], right[...])
        kept = pl.ds(pl.multiple_of(offset + 128 * j, 128), 128)
        half[kept, :NQ] = (one[:, :NQ] - two[:, NQ:]).astype(BF16)
        half[kept, NQ:] = (one[:, NQ:] + two[:, :NQ]).astype(BF16)


def early_kernel(cells, phi, right, half, wide, data):
    wide[...] = cells[...].astype(F32)
    forward_rows(wide, phi, right, data, half, own_core() * 256, 0)


def main_kernel(
    other, cells, early, right, phi, left, prop_far, back_far, out,
    wide, data, half, spec, turn, fold, last, rows_in, rows_out, prop, back, sems,
):
    far = ((prop_far, prop), (back_far, back))
    copies = [pltpu.make_async_copy(a, b, sems.at[k]) for k, (a, b) in enumerate(far)]
    for copy in copies:
        copy.start()
    place = lax.axis_index("beam")
    core = own_core()
    wide[...] = other[...].astype(F32)
    start = core * 256
    half[pl.ds(pl.multiple_of(start, 256), 256), :] = early[...]
    forward_rows(wide, phi, right, data, half, 256 - start, 256 - start)
    side = pl.ds(pl.multiple_of(place // 16 % 2 * HALF, HALF), HALF)
    copies[0].wait()
    for j in range(3):
        rows = slice(128 * j, 128 * j + 128)
        low = slice(NQ + 128 * j, NQ + 128 * j + 128)
        one = dot(left[rows, :], half[...])
        two = dot(left[low, :], half[...])
        re = one[:, :NQ] - two[:, NQ:]
        im = one[:, NQ:] + two[:, :NQ]
        pr = prop[rows, :NQ]
        pi = prop[rows, NQ:]
        new_r = re * pr - im * pi
        new_i = re * pi + im * pr
        spec[rows, :NQ] = new_r.astype(BF16)
        spec[rows, NQ:] = new_i.astype(BF16)
        turn[rows, :NQ] = new_i.astype(BF16)
        turn[rows, NQ:] = (-new_r).astype(BF16)
        at_r = dot_t(spec[rows, :], right[side, :])
        at_i = dot_t(turn[rows, :], right[side, :])
        fold[rows, :HALF] = at_r.astype(BF16)
        fold[rows, HALF:] = at_i.astype(BF16)
        fold[low, :HALF] = (-at_i).astype(BF16)
        fold[low, HALF:] = at_r.astype(BF16)
    copies[1].wait()
    for source in range(2):
        if source == 1:
            wide[...] = cells[...].astype(F32)
        first = 256 - start if source == 0 else start
        for j in range(2):
            rows = pl.ds(pl.multiple_of(first + 128 * j, 128), 128)
            wave = dot(back[rows, :], fold[...])
            for q in range(2):
                cos, sin = phase_factor(wide[pl.ds(8 + 2 * j + q, 128, stride=ROWS), :])
                re = wave[:, 128 * q : 128 * q + 128]
                im = wave[:, HALF + 128 * q : HALF + 128 * q + 128]
                last[rows, 128 * q : 128 * q + 128] = (re * cos - im * sin).astype(BF16)
                last[rows, HALF + 128 * q : HALF + 128 * q + 128] = (re * sin + im * cos).astype(BF16)
    band = pl.multiple_of(place // PEERS * 2 * PEERS, 2 * PEERS)
    one = dot(left[pl.ds(band, 2 * PEERS), :], last[...])
    two = dot(left[pl.ds(NQ + band, 2 * PEERS), :], last[...])
    parts = (one[:, :HALF] - two[:, HALF:], one[:, HALF:] + two[:, :HALF])
    for q in range(4):
        rows_in[...] = parts[q // 2][:, 128 * (q % 2) : 128 * (q % 2) + 128]
        for row in range(2):
            rows_out[pl.ds(2 * q + row, PEERS, stride=8), :] = rows_in[pl.ds(row, PEERS, stride=2), :]
    out[...] = rows_out[...].astype(BF16)


def final_kernel(parts, final, prop, out, wide, data):
    wide[...] = parts[...].astype(F32)
    for h in range(2):
        for q in range(4):
            for row in range(2):
                own = wide[pl.ds(128 * h + 2 * q + row, 16, stride=8), :]
                cols = slice(512 * h + 128 * q, 512 * h + 128 * q + 128)
                data[16 * row : 16 * row + 16, cols] = own.astype(BF16)
    acc = dot(data[...], final[...])
    for row in range(2):
        re = acc[16 * row : 16 * row + 16, :BAND]
        im = acc[16 * row : 16 * row + 16, BAND:]
        pr = prop[row : row + 1, :BAND]
        pi = prop[row : row + 1, BAND:]
        cols = slice(row * BAND, row * BAND + BAND)
        out[0, :, cols] = re * pr - im * pi
        out[1, :, cols] = re * pi + im * pr


VMEM = pl.BlockSpec(memory_space=pltpu.VMEM)
LIMIT = pltpu.CompilerParams(vmem_limit_bytes=16 * 1024 * 1024)
FAR = pl.BlockSpec(memory_space=pltpu.HBM)


def prepare(beams, right, back, chirp):
    return pl.pallas_call(
        prepare_kernel,
        in_specs=[VMEM] * 5,
        out_specs=[VMEM] * 2,
        out_shape=[
            pltpu.VMEM((G, 2 * G), BF16),
            pltpu.HBM((NQ, 2 * NQ), F32),
        ],
        compiler_params=LIMIT,
        name="prepare",
    )(beams, right, back, chirp, chirp.T)


def early(cells, phi, right):
    return pl.pallas_call(
        early_kernel,
        in_specs=[VMEM] * 3,
        out_specs=VMEM,
        out_shape=pltpu.VMEM((G // 2, 2 * NQ), BF16),
        scratch_shapes=[
            pltpu.VMEM((cells.shape[0], 128), F32),
            pltpu.VMEM((G // 2, 2 * G), BF16),
        ],
        compiler_params=LIMIT,
        name="early",
    )(cells, phi, right)


def main(near, far):
    rows = near[0].shape[0]
    return pl.pallas_call(
        main_kernel,
        in_specs=[VMEM] * 6 + [FAR] * 2,
        out_specs=VMEM,
        out_shape=jax.ShapeDtypeStruct((8 * PEERS, 128), BF16),
        scratch_shapes=[
            pltpu.VMEM((rows, 128), F32),
            pltpu.VMEM((G // 2, 2 * G), BF16),
            pltpu.VMEM((G, 2 * NQ), BF16),
            pltpu.VMEM((NQ, 2 * NQ), BF16),
            pltpu.VMEM((NQ, 2 * NQ), BF16),
            pltpu.VMEM((2 * NQ, 2 * HALF), BF16),
            pltpu.VMEM((G, 2 * HALF), BF16),
            pltpu.VMEM((2 * PEERS, 128), F32),
            pltpu.VMEM((8 * PEERS, 128), F32),
        ]
        + [pltpu.VMEM(a.shape, a.dtype) for a in far]
        + [pltpu.SemaphoreType.DMA((2,))],
        compiler_params=LIMIT,
        name="propagate",
    )(*near, *far)


def finish_table(right, sent):
    return pl.pallas_call(
        finish_table_kernel,
        in_specs=[VMEM, FAR],
        out_specs=VMEM,
        out_shape=jax.ShapeDtypeStruct((2 * G, 2 * BAND), BF16),
        compiler_params=LIMIT,
        name="finish_table",
    )(right, sent)


placed = pltpu.with_memory_space_constraint


def finish(parts, final, prop):
    return pl.pallas_call(
        final_kernel,
        in_specs=[VMEM] * 3,
        out_specs=VMEM,
        out_shape=jax.ShapeDtypeStruct((2, 16, 2 * BAND), F32),
        scratch_shapes=[pltpu.VMEM((8 * PEERS, 128), F32), pltpu.VMEM((32, 1024), BF16)],
        compiler_params=LIMIT,
        name="finish",
    )(parts, final, prop)


def own_coefficients(vectors, site):
    wave_x = vectors[:, 0]
    wave_y = vectors[:, 1]
    phases = jnp.mod(site[0] * wave_x + site[1] * wave_y, G)
    angle = -2.0 * math.pi / G * phases.astype(F32)
    weight = jnp.exp(-(wave_x * wave_x + wave_y * wave_y).astype(F32) * (8.0 / (BAND * BAND)))
    weight = weight * (1.0 / math.sqrt(vectors.shape[0]))
    coef_r = (weight * jnp.cos(angle)).astype(BF16).astype(F32) * G
    coef_i = (weight * jnp.sin(angle)).astype(BF16).astype(F32) * G
    offset = BAND // 2
    rows = [(wave_x + offset).astype(F32), (wave_y + offset).astype(F32), coef_r, coef_i]
    return jnp.concatenate([jnp.stack(rows, 0), jnp.zeros((4, vectors.shape[0]), F32)], 0)


def band_rows(first):
    fx = first + jnp.arange(2, dtype=jnp.int32) - BAND // 2
    fy = jnp.arange(BAND, dtype=jnp.int32) - BAND // 2
    squared = fx[:, None] * fx[:, None] + fy[None, :] * fy[None, :]
    inside = (9 * squared < G * G).astype(F32)
    angle = -2.0 * math.pi / (G * G) * jnp.mod(CHIRP_RATE * squared, G * G).astype(F32)
    return jnp.concatenate([inside * jnp.cos(angle), inside * jnp.sin(angle)], 1)


def message_kernel(cells, out, rows, block):
    wide = cells[...].astype(F32)
    own = jnp.where(own_core() == 0, wide[:, : 2 * G], wide[:, 2 * G :])
    for k in range(8):
        rows[k : k + 1, :] = own[0:1, 128 * k : 128 * k + 128]
    size = 8 * ROWS
    for h in range(2):
        for k in range(4):
            at = G * (k // 2) + HALF * h + 128 * (k % 2)
            rows[8 + k : 9 + k, :] = own[1:2, at : at + 128]
        for m in range(8):
            block[ROWS * m : ROWS * m + ROWS, :] = rows[...]
        copies = block[...].astype(BF16)
        for t in range(h, 8, 2):
            out[2 * t * size : (2 * t + 1) * size, :] = copies
            out[(2 * t + 1) * size : (2 * t + 2) * size, :] = copies


def message(potential):
    return pl.pallas_call(
        message_kernel,
        in_specs=[VMEM],
        out_specs=VMEM,
        out_shape=jax.ShapeDtypeStruct((128 * ROWS, 128), BF16),
        scratch_shapes=[pltpu.VMEM((ROWS, 128), F32), pltpu.VMEM((8 * ROWS, 128), F32)],
        compiler_params=LIMIT,
        name="message",
    )(potential)


def near_groups(peers):
    groups = []
    for turn in range(2):
        for core in range(2):
            groups.append([4 * k + 2 * ((k + turn) % 2) + core for k in range(peers)])
    return groups


def local(potential, wave_vectors, probe_sites):
    right, left, back, chirp = (jnp.asarray(t) for t in constant_tables())
    peers = lax.axis_size("beam")
    position = lax.axis_index("beam")
    group = lax.axis_index("grp")
    mine = message(potential).reshape(peers, ROWS // 2, 2, 128)
    cells = lax.all_to_all(
        mine, ("beam", "grp"), 0, 0, tiled=True, axis_index_groups=near_groups(peers)
    )
    site = lax.dynamic_index_in_dim(probe_sites, group * 16 + position % 16, 0, keepdims=False)
    beams = own_coefficients(wave_vectors, site)
    made = prepare(beams, right, back, chirp)
    cells, phi, prop = lax.optimization_barrier((cells, *made))
    cells = cells.reshape(peers * ROWS, 128)
    other = lax.ppermute(cells, "grp", [(0, 1), (1, 0), (2, 3), (3, 2)])
    cells, right_near, phi, left = (placed(a, pltpu.VMEM) for a in (cells, right, phi, left))
    first = placed(early(cells, phi, right_near), pltpu.VMEM)
    near = (placed(other, pltpu.VMEM), cells, first, right_near, phi, left)
    far = [placed(a, pltpu.HBM) for a in (prop, back)]
    sent = main(near, far)
    runs = [list(range(k, k + PEERS)) for k in range(0, peers, PEERS)]
    parts = lax.all_to_all(
        sent.reshape(PEERS, 8, 128), "beam", 0, 0, tiled=True, axis_index_groups=runs
    )
    final = finish_table(right, sent)
    return finish(parts.reshape(8 * PEERS, 128), final, band_rows(2 * position))


def solution(mesh):
    in_specs = (P(None, "beam"), P(), P())
    out_specs = P(None, "grp", "beam")
    return jax.shard_map(local, mesh=mesh, in_specs=in_specs, out_specs=out_specs, check_vma=False)
```

```python
import math

import jax
import jax.numpy as jnp
import numpy as np
from jax import lax
from jax.experimental import pallas as pl
from jax.experimental.pallas import tpu as pltpu
from jax.sharding import PartitionSpec as P

G = 512
BAND = 256
NQ = 384
PHASE_SCALE = 2.5
CHIRP_RATE = 20
PEERS = 32
HALF = 256
ROWS = 12

F32 = jnp.float32
BF16 = jnp.bfloat16


def frequencies():
    reach = math.isqrt((G * G - 1) // 9)
    band = np.arange(-BAND // 2, BAND // 2)
    high = np.arange(BAND // 2, reach + 1)
    low = np.arange(-reach, -BAND // 2)
    return np.concatenate([band, high, low])


def forward_table(places):
    freqs = frequencies()
    phases = np.mod(freqs[None, :] * places[:, None], G)
    angle = 2.0 * np.pi / G * phases
    table = np.zeros((2, places.shape[0], NQ), np.float64)
    table[0, :, : freqs.size] = np.cos(angle) / np.sqrt(G)
    table[1, :, : freqs.size] = -np.sin(angle) / np.sqrt(G)
    return table


def constant_tables():
    places = np.arange(G)
    permuted = (4 * np.arange(G // 4)[None, :] + np.arange(4)[:, None]).reshape(-1)
    natural = forward_table(places)
    shuffled = forward_table(permuted)
    right = np.concatenate([natural[0], natural[1]], 1)
    left = np.stack([shuffled[0].T, shuffled[1].T], 0).reshape(2, 3, 128, G)
    left = left.swapaxes(0, 1).reshape(2 * NQ, G)
    back = np.concatenate([shuffled[0], -shuffled[1]], 1)
    freqs = frequencies()
    squared = np.full((NQ,), 1.0e9)
    squared[: freqs.size] = freqs * freqs
    angle = np.zeros((NQ,))
    angle[: freqs.size] = -2.0 * np.pi / (G * G) * np.mod(CHIRP_RATE * freqs * freqs, G * G)
    chirp = np.stack([np.cos(angle), np.sin(angle), squared], 0)
    lanes = np.zeros((8, NQ))
    lanes[:3] = chirp
    return (
        right.astype(BF16),
        left.astype(BF16),
        back.astype(BF16),
        lanes.astype(np.float32),
    )


def half_turn_fits():
    nodes = 0.5 * np.cos(np.pi * (np.arange(400) + 0.5) / 400)
    square = nodes * nodes
    root = math.sqrt(2.0)
    sine = root * np.sin(np.pi * nodes) / nodes
    cosine = root * np.cos(np.pi * nodes)
    fit = np.polynomial.Polynomial.fit
    return (
        [float(v) for v in fit(square, sine, 4, domain=[0, 0.25]).convert().coef],
        [float(v) for v in fit(square, cosine, 4, domain=[0, 0.25]).convert().coef],
    )


SINE, COSINE = half_turn_fits()


def horner(coefs, x):
    total = coefs[-1]
    for coef in coefs[-2::-1]:
        total = total * x + coef
    return total


def phase_factor(cells):
    turns = cells * (PHASE_SCALE / (2.0 * math.pi))
    rest = turns - jnp.round(turns)
    square = rest * rest
    sine = rest * horner(SINE, square)
    cosine = horner(COSINE, square)
    return 1.0 - sine * sine, sine * cosine


def own_core():
    return lax.axis_index("grp") % 2


def dot(a, b):
    return jnp.dot(a, b, preferred_element_type=F32)


def dot_t(a, b):
    return lax.dot_general(a, b, (((1,), (1,)), ((), ())), preferred_element_type=F32)


def prepare_kernel(beams, right, back, chirp, chirp_t, phi, prop):
    index = lax.broadcasted_iota(jnp.int32, (BAND, G), 0).astype(F32)
    on_x = index == beams[0:1, :]
    on_y = jnp.where(index == beams[1:2, :], 1.0, 0.0).astype(BF16)
    grid_r = dot_t(jnp.where(on_x, beams[2:3, :], 0.0).astype(BF16), on_y)
    grid_i = dot_t(jnp.where(on_x, beams[3:4, :], 0.0).astype(BF16), on_y)
    grid = jnp.concatenate([grid_r, grid_i], 1).astype(BF16)
    by_r = dot(back[:, 0:BAND], grid)
    by_i = dot(back[:, NQ : NQ + BAND], grid)
    mid_r = by_r[:, :BAND] - by_i[:, BAND:]
    mid_i = by_r[:, BAND:] + by_i[:, :BAND]
    band_r = right[:, 0:BAND]
    band_i = right[:, NQ : NQ + BAND]
    both = jnp.concatenate([band_r, band_i], 1)
    phi[:, :G] = dot_t(jnp.concatenate([mid_r, mid_i], 1).astype(BF16), both).astype(BF16)
    phi[:, G:] = dot_t(jnp.concatenate([mid_i, -mid_r], 1).astype(BF16), both).astype(BF16)
    inside = chirp_t[:, 2:3] + chirp[2:3, :] < (G * G - 1) // 9 + 0.5
    xr = chirp_t[:, 0:1]
    xi = chirp_t[:, 1:2]
    yr = chirp[0:1, :]
    yi = chirp[1:2, :]
    prop[:, :NQ] = jnp.where(inside, xr * yr - xi * yi, 0.0)
    prop[:, NQ:] = jnp.where(inside, xr * yi + xi * yr, 0.0)


def finish_table_kernel(right, sent, final):
    for h in range(2):
        rows = slice(h * HALF, h * HALF + HALF)
        top = slice(2 * h * HALF, (2 * h + 1) * HALF)
        low = slice((2 * h + 1) * HALF, (2 * h + 2) * HALF)
        final[top, :BAND] = right[rows, 0:BAND]
        final[top, BAND:] = right[rows, NQ : NQ + BAND]
        final[low, :BAND] = -right[rows, NQ : NQ + BAND]
        final[low, BAND:] = right[rows, 0:BAND]


def forward_rows(wide, phi, right, data, half, first, offset):
    for j in range(2):
        rows = slice(256 * j, 256 * j + 128)
        low = slice(256 * j + 128, 256 * j + 256)
        probe = pl.ds(pl.multiple_of(first + 128 * j, 128), 128)
        for h in range(4):
            cos, sin = phase_factor(wide[pl.ds(4 * j + h, 128, stride=ROWS), :])
            pr = phi[probe, 128 * h : 128 * h + 128].astype(F32)
            pi = phi[probe, G + 128 * h : G + 128 * h + 128].astype(F32)
            data[rows, 128 * h : 128 * h + 128] = (pr * cos - pi * sin).astype(BF16)
            data[low, 128 * h : 128 * h + 128] = (pr * sin + pi * cos).astype(BF16)
        both = dot(data[256 * j : 256 * j + 256, :], right[...])
        kept = pl.ds(pl.multiple_of(offset + 128 * j, 128), 128)
        half[kept, :NQ] = (both[:128, :NQ] - both[128:, NQ:]).astype(BF16)
        half[kept, NQ:] = (both[:128, NQ:] + both[128:, :NQ]).astype(BF16)


def second_factors(wide, factors, j):
    rows = slice(128 * j, 128 * j + 128)
    for q in range(2):
        cos, sin = phase_factor(wide[pl.ds(8 + 2 * j + q, 128, stride=ROWS), :])
        factors[rows, 128 * q : 128 * q + 128] = cos
        factors[rows, HALF + 128 * q : HALF + 128 * q + 128] = sin


def early_kernel(cells, phi, right, half, factors, wide, data):
    wide[...] = cells[...].astype(F32)
    forward_rows(wide, phi, right, data, half, own_core() * 256, 0)
    for j in range(2):
        second_factors(wide, factors, j)


def main_kernel(
    other, early, own_factors, right, phi, prop, back, left_far, out,
    wide, data, half, spec, fold, last, factors, rows_in, rows_out, left, sem,
):
    copy = pltpu.make_async_copy(left_far, left, sem)
    copy.start()
    place = lax.axis_index("beam")
    core = own_core()
    wide[...] = other[...].astype(F32)
    start = core * 256
    half[pl.ds(pl.multiple_of(start, 256), 256), :] = early[...]
    forward_rows(wide, phi, right, data, half, 256 - start, 256 - start)
    side = pl.ds(pl.multiple_of(place // 16 % 2 * HALF, HALF), HALF)
    copy.wait()
    for j in range(3):
        rows = slice(128 * j, 128 * j + 128)
        low = slice(NQ + 128 * j, NQ + 128 * j + 128)
        both = dot(left[256 * j : 256 * j + 256, :], half[...])
        if j < 2:
            second_factors(wide, factors, j)
        re = both[:128, :NQ] - both[128:, NQ:]
        im = both[:128, NQ:] + both[128:, :NQ]
        pr = prop[rows, :NQ]
        pi = prop[rows, NQ:]
        new_r = re * pr - im * pi
        new_i = re * pi + im * pr
        spec[256 * j : 256 * j + 128, :NQ] = new_r.astype(BF16)
        spec[256 * j : 256 * j + 128, NQ:] = new_i.astype(BF16)
        spec[256 * j + 128 : 256 * j + 256, :NQ] = new_i.astype(BF16)
        spec[256 * j + 128 : 256 * j + 256, NQ:] = (-new_r).astype(BF16)
        both = dot_t(spec[256 * j : 256 * j + 256, :], right[side, :])
        fold[rows, :HALF] = both[:128].astype(BF16)
        fold[rows, HALF:] = both[128:].astype(BF16)
        fold[low, :HALF] = (-both[128:]).astype(BF16)
        fold[low, HALF:] = both[:128].astype(BF16)
    for table, first in ((factors, 256 - start), (own_factors, start)):
        rows = pl.ds(pl.multiple_of(first, 256), 256)
        wave = dot(back[rows, :], fold[...])
        cos = table[:, :HALF]
        sin = table[:, HALF:]
        last[rows, :HALF] = (wave[:, :HALF] * cos - wave[:, HALF:] * sin).astype(BF16)
        last[rows, HALF:] = (wave[:, :HALF] * sin + wave[:, HALF:] * cos).astype(BF16)
    part = place // PEERS
    band = pl.multiple_of(part // 2 * 256 + part % 2 * 64, 2 * PEERS)
    one = dot(left[pl.ds(band, 2 * PEERS), :], last[...])
    two = dot(left[pl.ds(band + 128, 2 * PEERS), :], last[...])
    parts = (one[:, :HALF] - two[:, HALF:], one[:, HALF:] + two[:, :HALF])
    for q in range(4):
        rows_in[...] = parts[q // 2][:, 128 * (q % 2) : 128 * (q % 2) + 128]
        for row in range(2):
            rows_out[pl.ds(2 * q + row, PEERS, stride=8), :] = rows_in[pl.ds(row, PEERS, stride=2), :]
    out[...] = rows_out[...].astype(BF16)


def final_kernel(parts, final, prop, out, wide, data):
    wide[...] = parts[...].astype(F32)
    for h in range(2):
        for q in range(4):
            for row in range(2):
                own = wide[pl.ds(128 * h + 2 * q + row, 16, stride=8), :]
                cols = slice(512 * h + 128 * q, 512 * h + 128 * q + 128)
                data[16 * row : 16 * row + 16, cols] = own.astype(BF16)
    acc = dot(data[...], final[...])
    for row in range(2):
        re = acc[16 * row : 16 * row + 16, :BAND]
        im = acc[16 * row : 16 * row + 16, BAND:]
        pr = prop[row : row + 1, :BAND]
        pi = prop[row : row + 1, BAND:]
        cols = slice(row * BAND, row * BAND + BAND)
        out[0, :, cols] = re * pr - im * pi
        out[1, :, cols] = re * pi + im * pr


VMEM = pl.BlockSpec(memory_space=pltpu.VMEM)
LIMIT = pltpu.CompilerParams(vmem_limit_bytes=16 * 1024 * 1024)
FAR = pl.BlockSpec(memory_space=pltpu.HBM)


def prepare(beams, right, back, chirp):
    return pl.pallas_call(
        prepare_kernel,
        in_specs=[VMEM] * 5,
        out_specs=[VMEM] * 2,
        out_shape=[
            pltpu.VMEM((G, 2 * G), BF16),
            pltpu.HBM((NQ, 2 * NQ), F32),
        ],
        compiler_params=LIMIT,
        name="prepare",
    )(beams, right, back, chirp, chirp.T)


def early(cells, phi, right):
    return pl.pallas_call(
        early_kernel,
        in_specs=[VMEM] * 3,
        out_specs=[VMEM] * 2,
        out_shape=[pltpu.VMEM((G // 2, 2 * NQ), BF16), pltpu.VMEM((G // 2, 2 * HALF), F32)],
        scratch_shapes=[
            pltpu.VMEM((cells.shape[0], 128), F32),
            pltpu.VMEM((G, G), BF16),
        ],
        compiler_params=LIMIT,
        name="early",
    )(cells, phi, right)


def main(near, left):
    rows = near[0].shape[0]
    return pl.pallas_call(
        main_kernel,
        in_specs=[VMEM] * 7 + [FAR],
        out_specs=VMEM,
        out_shape=jax.ShapeDtypeStruct((8 * PEERS, 128), BF16),
        scratch_shapes=[
            pltpu.VMEM((rows, 128), F32),
            pltpu.VMEM((G, G), BF16),
            pltpu.VMEM((G, 2 * NQ), BF16),
            pltpu.VMEM((2 * NQ, 2 * NQ), BF16),
            pltpu.VMEM((2 * NQ, 2 * HALF), BF16),
            pltpu.VMEM((G, 2 * HALF), BF16),
            pltpu.VMEM((G // 2, 2 * HALF), F32),
            pltpu.VMEM((2 * PEERS, 128), F32),
            pltpu.VMEM((8 * PEERS, 128), F32),
            pltpu.VMEM(left.shape, BF16),
            pltpu.SemaphoreType.DMA,
        ],
        compiler_params=LIMIT,
        name="propagate",
    )(*near, left)


def finish_table(right, sent):
    return pl.pallas_call(
        finish_table_kernel,
        in_specs=[VMEM, FAR],
        out_specs=VMEM,
        out_shape=jax.ShapeDtypeStruct((2 * G, 2 * BAND), BF16),
        compiler_params=LIMIT,
        name="finish_table",
    )(right, sent)


placed = pltpu.with_memory_space_constraint


def finish(parts, final, prop):
    return pl.pallas_call(
        final_kernel,
        in_specs=[VMEM] * 3,
        out_specs=VMEM,
        out_shape=jax.ShapeDtypeStruct((2, 16, 2 * BAND), F32),
        scratch_shapes=[pltpu.VMEM((8 * PEERS, 128), F32), pltpu.VMEM((32, 1024), BF16)],
        compiler_params=LIMIT,
        name="finish",
    )(parts, final, prop)


def own_coefficients(vectors, site):
    wave_x = vectors[:, 0]
    wave_y = vectors[:, 1]
    phases = jnp.mod(site[0] * wave_x + site[1] * wave_y, G)
    angle = -2.0 * math.pi / G * phases.astype(F32)
    weight = jnp.exp(-(wave_x * wave_x + wave_y * wave_y).astype(F32) * (8.0 / (BAND * BAND)))
    weight = weight * (1.0 / math.sqrt(vectors.shape[0]))
    coef_r = (weight * jnp.cos(angle)).astype(BF16).astype(F32) * G
    coef_i = (weight * jnp.sin(angle)).astype(BF16).astype(F32) * G
    offset = BAND // 2
    rows = [(wave_x + offset).astype(F32), (wave_y + offset).astype(F32), coef_r, coef_i]
    return jnp.concatenate([jnp.stack(rows, 0), jnp.zeros((4, vectors.shape[0]), F32)], 0)


def band_rows(first):
    fx = first + jnp.arange(2, dtype=jnp.int32) - BAND // 2
    fy = jnp.arange(BAND, dtype=jnp.int32) - BAND // 2
    squared = fx[:, None] * fx[:, None] + fy[None, :] * fy[None, :]
    inside = (9 * squared < G * G).astype(F32)
    angle = -2.0 * math.pi / (G * G) * jnp.mod(CHIRP_RATE * squared, G * G).astype(F32)
    return jnp.concatenate([inside * jnp.cos(angle), inside * jnp.sin(angle)], 1)


def message_kernel(cells, out, rows, block):
    wide = cells[...].astype(F32)
    own = jnp.where(own_core() == 0, wide[:, : 2 * G], wide[:, 2 * G :])
    for k in range(8):
        rows[k : k + 1, :] = own[0:1, 128 * k : 128 * k + 128]
    size = 8 * ROWS
    for h in range(2):
        for k in range(4):
            at = G * (k // 2) + HALF * h + 128 * (k % 2)
            rows[8 + k : 9 + k, :] = own[1:2, at : at + 128]
        for m in range(8):
            block[ROWS * m : ROWS * m + ROWS, :] = rows[...]
        copies = block[...].astype(BF16)
        for t in range(h, 8, 2):
            out[2 * t * size : (2 * t + 1) * size, :] = copies
            out[(2 * t + 1) * size : (2 * t + 2) * size, :] = copies


def message(potential):
    return pl.pallas_call(
        message_kernel,
        in_specs=[VMEM],
        out_specs=VMEM,
        out_shape=jax.ShapeDtypeStruct((128 * ROWS, 128), BF16),
        scratch_shapes=[pltpu.VMEM((ROWS, 128), F32), pltpu.VMEM((8 * ROWS, 128), F32)],
        compiler_params=LIMIT,
        name="message",
    )(potential)


def near_groups(peers):
    groups = []
    for turn in range(2):
        for core in range(2):
            groups.append([4 * k + 2 * ((k + turn) % 2) + core for k in range(peers)])
    return groups


def local(potential, wave_vectors, probe_sites):
    right, left, back, chirp = (jnp.asarray(t) for t in constant_tables())
    peers = lax.axis_size("beam")
    position = lax.axis_index("beam")
    group = lax.axis_index("grp")
    mine = message(potential).reshape(peers, ROWS // 2, 2, 128)
    cells = lax.all_to_all(
        mine, ("beam", "grp"), 0, 0, tiled=True, axis_index_groups=near_groups(peers)
    )
    site = lax.dynamic_index_in_dim(probe_sites, group * 16 + position % 16, 0, keepdims=False)
    beams = own_coefficients(wave_vectors, site)
    made = prepare(beams, right, back, chirp)
    cells, phi, prop = lax.optimization_barrier((cells, *made))
    cells = cells.reshape(peers * ROWS, 128)
    other = lax.ppermute(cells, "grp", [(0, 1), (1, 0), (2, 3), (3, 2)])
    cells, right_near, phi = (placed(a, pltpu.VMEM) for a in (cells, right, phi))
    first, factors = (placed(a, pltpu.VMEM) for a in early(cells, phi, right_near))
    other, prop, back = (placed(a, pltpu.VMEM) for a in (other, prop, back))
    near = (other, first, factors, right_near, phi, prop, back)
    sent = main(near, placed(left, pltpu.HBM))
    runs = [list(range(k, k + PEERS)) for k in range(0, peers, PEERS)]
    parts = lax.all_to_all(
        sent.reshape(PEERS, 8, 128), "beam", 0, 0, tiled=True, axis_index_groups=runs
    )
    final = finish_table(right, sent)
    return finish(parts.reshape(8 * PEERS, 128), final, band_rows(2 * position))


def solution(mesh):
    in_specs = (P(None, "beam"), P(), P())
    out_specs = P(None, "grp", "beam")
    return jax.shard_map(local, mesh=mesh, in_specs=in_specs, out_specs=out_specs, check_vma=False)
```

```python
import math

import jax
import jax.numpy as jnp
import numpy as np
from jax import lax
from jax.experimental import pallas as pl
from jax.experimental.pallas import tpu as pltpu
from jax.sharding import PartitionSpec as P

G = 512
BAND = 256
NQ = 384
PHASE_SCALE = 2.5
CHIRP_RATE = 20
PEERS = 32
HALF = 256
ROWS = 12

F32 = jnp.float32
BF16 = jnp.bfloat16


def frequencies():
    reach = math.isqrt((G * G - 1) // 9)
    band = np.arange(-BAND // 2, BAND // 2)
    high = np.arange(BAND // 2, reach + 1)
    low = np.arange(-reach, -BAND // 2)
    return np.concatenate([band, high, low])


def forward_table(places):
    freqs = frequencies()
    phases = np.mod(freqs[None, :] * places[:, None], G)
    angle = 2.0 * np.pi / G * phases
    table = np.zeros((2, places.shape[0], NQ), np.float64)
    table[0, :, : freqs.size] = np.cos(angle) / np.sqrt(G)
    table[1, :, : freqs.size] = -np.sin(angle) / np.sqrt(G)
    return table


def constant_tables():
    places = np.arange(G)
    permuted = (4 * np.arange(G // 4)[None, :] + np.arange(4)[:, None]).reshape(-1)
    natural = forward_table(places)
    shuffled = forward_table(permuted)
    right = np.concatenate([natural[0], natural[1]], 1)
    left = np.stack([shuffled[0].T, shuffled[1].T], 0).reshape(2, 3, 128, G)
    left = left.swapaxes(0, 1).reshape(2 * NQ, G)
    back = np.concatenate([shuffled[0], -shuffled[1]], 1)
    freqs = frequencies()
    squared = np.full((NQ,), 1.0e9)
    squared[: freqs.size] = freqs * freqs
    angle = np.zeros((NQ,))
    angle[: freqs.size] = -2.0 * np.pi / (G * G) * np.mod(CHIRP_RATE * freqs * freqs, G * G)
    chirp = np.stack([np.cos(angle), np.sin(angle), squared], 0)
    lanes = np.zeros((8, NQ))
    lanes[:3] = chirp
    return (
        right.astype(BF16),
        left.astype(BF16),
        back.astype(BF16),
        lanes.astype(np.float32),
    )


def half_turn_fits():
    nodes = 0.5 * np.cos(np.pi * (np.arange(400) + 0.5) / 400)
    square = nodes * nodes
    root = math.sqrt(2.0)
    sine = root * np.sin(np.pi * nodes) / nodes
    cosine = root * np.cos(np.pi * nodes)
    fit = np.polynomial.Polynomial.fit
    return (
        [float(v) for v in fit(square, sine, 4, domain=[0, 0.25]).convert().coef],
        [float(v) for v in fit(square, cosine, 4, domain=[0, 0.25]).convert().coef],
    )


SINE, COSINE = half_turn_fits()


def horner(coefs, x):
    total = coefs[-1]
    for coef in coefs[-2::-1]:
        total = total * x + coef
    return total


def phase_factor(cells):
    turns = cells * (PHASE_SCALE / (2.0 * math.pi))
    rest = turns - jnp.round(turns)
    square = rest * rest
    sine = rest * horner(SINE, square)
    cosine = horner(COSINE, square)
    return 1.0 - sine * sine, sine * cosine


def own_core():
    return lax.axis_index("grp") % 2


def dot(a, b):
    return jnp.dot(a, b, preferred_element_type=F32)


def dot_t(a, b):
    return lax.dot_general(a, b, (((1,), (1,)), ((), ())), preferred_element_type=F32)


def prepare_kernel(beams, right, back, chirp, chirp_t, phi, prop, final):
    index = lax.broadcasted_iota(jnp.int32, (BAND, G), 0).astype(F32)
    on_x = index == beams[0:1, :]
    on_y = jnp.where(index == beams[1:2, :], 1.0, 0.0).astype(BF16)
    grid_r = dot_t(jnp.where(on_x, beams[2:3, :], 0.0).astype(BF16), on_y)
    grid_i = dot_t(jnp.where(on_x, beams[3:4, :], 0.0).astype(BF16), on_y)
    grid = jnp.concatenate([grid_r, grid_i], 1).astype(BF16)
    by_r = dot(back[:, 0:BAND], grid)
    by_i = dot(back[:, NQ : NQ + BAND], grid)
    mid_r = by_r[:, :BAND] - by_i[:, BAND:]
    mid_i = by_r[:, BAND:] + by_i[:, :BAND]
    band_r = right[:, 0:BAND]
    band_i = right[:, NQ : NQ + BAND]
    both = jnp.concatenate([band_r, band_i], 1)
    phi[:, :G] = dot_t(jnp.concatenate([mid_r, mid_i], 1).astype(BF16), both).astype(BF16)
    phi[:, G:] = dot_t(jnp.concatenate([mid_i, -mid_r], 1).astype(BF16), both).astype(BF16)
    inside = chirp_t[:, 2:3] + chirp[2:3, :] < (G * G - 1) // 9 + 0.5
    xr = chirp_t[:, 0:1]
    xi = chirp_t[:, 1:2]
    yr = chirp[0:1, :]
    yi = chirp[1:2, :]
    prop[:, :NQ] = jnp.where(inside, xr * yr - xi * yi, 0.0)
    prop[:, NQ:] = jnp.where(inside, xr * yi + xi * yr, 0.0)
    for h in range(2):
        rows = slice(h * HALF, h * HALF + HALF)
        top = slice(2 * h * HALF, (2 * h + 1) * HALF)
        low = slice((2 * h + 1) * HALF, (2 * h + 2) * HALF)
        final[top, :BAND] = right[rows, 0:BAND]
        final[top, BAND:] = right[rows, NQ : NQ + BAND]
        final[low, :BAND] = -right[rows, NQ : NQ + BAND]
        final[low, BAND:] = right[rows, 0:BAND]


def forward_rows(wide, phi, right, data, half, first, offset):
    for j in range(2):
        rows = slice(256 * j, 256 * j + 128)
        low = slice(256 * j + 128, 256 * j + 256)
        probe = pl.ds(pl.multiple_of(first + 128 * j, 128), 128)
        for h in range(4):
            cos, sin = phase_factor(wide[pl.ds(4 * j + h, 128, stride=ROWS), :])
            pr = phi[probe, 128 * h : 128 * h + 128].astype(F32)
            pi = phi[probe, G + 128 * h : G + 128 * h + 128].astype(F32)
            data[rows, 128 * h : 128 * h + 128] = (pr * cos - pi * sin).astype(BF16)
            data[low, 128 * h : 128 * h + 128] = (pr * sin + pi * cos).astype(BF16)
        both = dot(data[256 * j : 256 * j + 256, :], right[...])
        kept = pl.ds(pl.multiple_of(offset + 128 * j, 128), 128)
        half[kept, :NQ] = (both[:128, :NQ] - both[128:, NQ:]).astype(BF16)
        half[kept, NQ:] = (both[:128, NQ:] + both[128:, :NQ]).astype(BF16)


def second_factors(wide, factors, j):
    rows = slice(128 * j, 128 * j + 128)
    for q in range(2):
        cos, sin = phase_factor(wide[pl.ds(8 + 2 * j + q, 128, stride=ROWS), :])
        factors[rows, 128 * q : 128 * q + 128] = cos
        factors[rows, HALF + 128 * q : HALF + 128 * q + 128] = sin


def early_kernel(cells, phi, right, half, factors, wide, data):
    wide[...] = cells[...].astype(F32)
    forward_rows(wide, phi, right, data, half, own_core() * 256, 0)
    for j in range(2):
        second_factors(wide, factors, j)


def main_kernel(
    other, early, own_factors, right, phi, prop, back, left_far, out,
    wide, data, half, spec, fold, last, factors, rows_in, rows_out, left, sem,
):
    copy = pltpu.make_async_copy(left_far, left, sem)
    copy.start()
    place = lax.axis_index("beam")
    core = own_core()
    wide[...] = other[...].astype(F32)
    start = core * 256
    half[pl.ds(pl.multiple_of(start, 256), 256), :] = early[...]
    forward_rows(wide, phi, right, data, half, 256 - start, 256 - start)
    side = pl.ds(pl.multiple_of(place // 16 % 2 * HALF, HALF), HALF)
    copy.wait()
    for j in range(3):
        rows = slice(128 * j, 128 * j + 128)
        low = slice(NQ + 128 * j, NQ + 128 * j + 128)
        both = dot(left[256 * j : 256 * j + 256, :], half[...])
        if j < 2:
            second_factors(wide, factors, j)
        re = both[:128, :NQ] - both[128:, NQ:]
        im = both[:128, NQ:] + both[128:, :NQ]
        pr = prop[rows, :NQ]
        pi = prop[rows, NQ:]
        new_r = re * pr - im * pi
        new_i = re * pi + im * pr
        spec[256 * j : 256 * j + 128, :NQ] = new_r.astype(BF16)
        spec[256 * j : 256 * j + 128, NQ:] = new_i.astype(BF16)
        spec[256 * j + 128 : 256 * j + 256, :NQ] = new_i.astype(BF16)
        spec[256 * j + 128 : 256 * j + 256, NQ:] = (-new_r).astype(BF16)
        both = dot_t(spec[256 * j : 256 * j + 256, :], right[side, :])
        fold[rows, :HALF] = both[:128].astype(BF16)
        fold[rows, HALF:] = both[128:].astype(BF16)
        fold[low, :HALF] = (-both[128:]).astype(BF16)
        fold[low, HALF:] = both[:128].astype(BF16)
    for table, first in ((factors, 256 - start), (own_factors, start)):
        rows = pl.ds(pl.multiple_of(first, 256), 256)
        wave = dot(back[rows, :], fold[...])
        cos = table[:, :HALF]
        sin = table[:, HALF:]
        last[rows, :HALF] = (wave[:, :HALF] * cos - wave[:, HALF:] * sin).astype(BF16)
        last[rows, HALF:] = (wave[:, :HALF] * sin + wave[:, HALF:] * cos).astype(BF16)
    part = place // PEERS
    band = pl.multiple_of(part // 2 * 256 + part % 2 * 64, 2 * PEERS)
    one = dot(left[pl.ds(band, 2 * PEERS), :], last[...])
    two = dot(left[pl.ds(band + 128, 2 * PEERS), :], last[...])
    parts = (one[:, :HALF] - two[:, HALF:], one[:, HALF:] + two[:, :HALF])
    for q in range(4):
        rows_in[...] = parts[q // 2][:, 128 * (q % 2) : 128 * (q % 2) + 128]
        for row in range(2):
            rows_out[pl.ds(2 * q + row, PEERS, stride=8), :] = rows_in[pl.ds(row, PEERS, stride=2), :]
    out[...] = rows_out[...].astype(BF16)


def final_kernel(parts, final, prop, out, wide, data):
    wide[...] = parts[...].astype(F32)
    for h in range(2):
        for q in range(4):
            for row in range(2):
                own = wide[pl.ds(128 * h + 2 * q + row, 16, stride=8), :]
                cols = slice(512 * h + 128 * q, 512 * h + 128 * q + 128)
                data[16 * row : 16 * row + 16, cols] = own.astype(BF16)
    acc = dot(data[...], final[...])
    for row in range(2):
        re = acc[16 * row : 16 * row + 16, :BAND]
        im = acc[16 * row : 16 * row + 16, BAND:]
        pr = prop[row : row + 1, :BAND]
        pi = prop[row : row + 1, BAND:]
        cols = slice(row * BAND, row * BAND + BAND)
        out[0, :, cols] = re * pr - im * pi
        out[1, :, cols] = re * pi + im * pr


VMEM = pl.BlockSpec(memory_space=pltpu.VMEM)
LIMIT = pltpu.CompilerParams(vmem_limit_bytes=16 * 1024 * 1024)
FAR = pl.BlockSpec(memory_space=pltpu.HBM)
placed = pltpu.with_memory_space_constraint


def prepare(beams, right, back, chirp):
    return pl.pallas_call(
        prepare_kernel,
        in_specs=[VMEM] * 5,
        out_specs=[VMEM] * 3,
        out_shape=[
            pltpu.VMEM((G, 2 * G), BF16),
            pltpu.HBM((NQ, 2 * NQ), F32),
            pltpu.VMEM((2 * G, 2 * BAND), BF16),
        ],
        compiler_params=LIMIT,
        name="prepare",
    )(beams, right, back, chirp, chirp.T)


def early(cells, phi, right):
    return pl.pallas_call(
        early_kernel,
        in_specs=[VMEM] * 3,
        out_specs=[VMEM] * 2,
        out_shape=[pltpu.VMEM((G // 2, 2 * NQ), BF16), pltpu.VMEM((G // 2, 2 * HALF), F32)],
        scratch_shapes=[
            pltpu.VMEM((cells.shape[0], 128), F32),
            pltpu.VMEM((G, G), BF16),
        ],
        compiler_params=LIMIT,
        name="early",
    )(cells, phi, right)


def main(near, left):
    rows = near[0].shape[0]
    return pl.pallas_call(
        main_kernel,
        in_specs=[VMEM] * 7 + [FAR],
        out_specs=VMEM,
        out_shape=jax.ShapeDtypeStruct((8 * PEERS, 128), BF16),
        scratch_shapes=[
            pltpu.VMEM((rows, 128), F32),
            pltpu.VMEM((G, G), BF16),
            pltpu.VMEM((G, 2 * NQ), BF16),
            pltpu.VMEM((2 * NQ, 2 * NQ), BF16),
            pltpu.VMEM((2 * NQ, 2 * HALF), BF16),
            pltpu.VMEM((G, 2 * HALF), BF16),
            pltpu.VMEM((G // 2, 2 * HALF), F32),
            pltpu.VMEM((2 * PEERS, 128), F32),
            pltpu.VMEM((8 * PEERS, 128), F32),
            pltpu.VMEM(left.shape, BF16),
            pltpu.SemaphoreType.DMA,
        ],
        compiler_params=LIMIT,
        name="propagate",
    )(*near, left)


def finish(parts, final, prop):
    return pl.pallas_call(
        final_kernel,
        in_specs=[VMEM] * 3,
        out_specs=VMEM,
        out_shape=jax.ShapeDtypeStruct((2, 16, 2 * BAND), F32),
        scratch_shapes=[pltpu.VMEM((8 * PEERS, 128), F32), pltpu.VMEM((32, 1024), BF16)],
        compiler_params=LIMIT,
        name="finish",
    )(parts, final, prop)


def own_coefficients(vectors, site):
    wave_x = vectors[:, 0]
    wave_y = vectors[:, 1]
    phases = jnp.mod(site[0] * wave_x + site[1] * wave_y, G)
    angle = -2.0 * math.pi / G * phases.astype(F32)
    weight = jnp.exp(-(wave_x * wave_x + wave_y * wave_y).astype(F32) * (8.0 / (BAND * BAND)))
    weight = weight * (1.0 / math.sqrt(vectors.shape[0]))
    coef_r = (weight * jnp.cos(angle)).astype(BF16).astype(F32) * G
    coef_i = (weight * jnp.sin(angle)).astype(BF16).astype(F32) * G
    offset = BAND // 2
    rows = [(wave_x + offset).astype(F32), (wave_y + offset).astype(F32), coef_r, coef_i]
    return jnp.concatenate([jnp.stack(rows, 0), jnp.zeros((4, vectors.shape[0]), F32)], 0)


def band_rows(first):
    fx = first + jnp.arange(2, dtype=jnp.int32) - BAND // 2
    fy = jnp.arange(BAND, dtype=jnp.int32) - BAND // 2
    squared = fx[:, None] * fx[:, None] + fy[None, :] * fy[None, :]
    inside = (9 * squared < G * G).astype(F32)
    angle = -2.0 * math.pi / (G * G) * jnp.mod(CHIRP_RATE * squared, G * G).astype(F32)
    return jnp.concatenate([inside * jnp.cos(angle), inside * jnp.sin(angle)], 1)


def message_kernel(cells, out, rows, block):
    wide = cells[...].astype(F32)
    own = jnp.where(own_core() == 0, wide[:, : 2 * G], wide[:, 2 * G :])
    for k in range(8):
        rows[k : k + 1, :] = own[0:1, 128 * k : 128 * k + 128]
    size = 8 * ROWS
    for h in range(2):
        for k in range(4):
            at = G * (k // 2) + HALF * h + 128 * (k % 2)
            rows[8 + k : 9 + k, :] = own[1:2, at : at + 128]
        for m in range(8):
            block[ROWS * m : ROWS * m + ROWS, :] = rows[...]
        copies = block[...].astype(BF16)
        for t in range(h, 8, 2):
            out[2 * t * size : (2 * t + 1) * size, :] = copies
            out[(2 * t + 1) * size : (2 * t + 2) * size, :] = copies


def message(potential):
    return pl.pallas_call(
        message_kernel,
        in_specs=[VMEM],
        out_specs=VMEM,
        out_shape=jax.ShapeDtypeStruct((128 * ROWS, 128), BF16),
        scratch_shapes=[pltpu.VMEM((ROWS, 128), F32), pltpu.VMEM((8 * ROWS, 128), F32)],
        compiler_params=LIMIT,
        name="message",
    )(potential)


def near_groups(peers):
    groups = []
    for turn in range(2):
        for core in range(2):
            groups.append([4 * k + 2 * ((k + turn) % 2) + core for k in range(peers)])
    return groups


def local(potential, wave_vectors, probe_sites):
    right, left, back, chirp = (jnp.asarray(t) for t in constant_tables())
    peers = lax.axis_size("beam")
    position = lax.axis_index("beam")
    group = lax.axis_index("grp")
    mine = message(potential).reshape(peers, ROWS // 2, 2, 128)
    cells = lax.all_to_all(
        mine, ("beam", "grp"), 0, 0, tiled=True, axis_index_groups=near_groups(peers)
    )
    site = lax.dynamic_index_in_dim(probe_sites, group * 16 + position % 16, 0, keepdims=False)
    beams = own_coefficients(wave_vectors, site)
    made = prepare(beams, right, back, chirp)
    band = band_rows(2 * position)
    cells, phi, prop, final, band = lax.optimization_barrier((cells, *made, band))
    cells = cells.reshape(peers * ROWS, 128)
    other = lax.ppermute(cells, "grp", [(0, 1), (1, 0), (2, 3), (3, 2)])
    cells, right_near, phi = (placed(a, pltpu.VMEM) for a in (cells, right, phi))
    first, factors = (placed(a, pltpu.VMEM) for a in early(cells, phi, right_near))
    other, prop, back = (placed(a, pltpu.VMEM) for a in (other, prop, back))
    near = (other, first, factors, right_near, phi, prop, back)
    sent = main(near, placed(left, pltpu.HBM))
    runs = [list(range(k, k + PEERS)) for k in range(0, peers, PEERS)]
    parts = lax.all_to_all(
        sent.reshape(PEERS, 8, 128), "beam", 0, 0, tiled=True, axis_index_groups=runs
    )
    return finish(parts.reshape(8 * PEERS, 128), placed(final, pltpu.VMEM), band)


def solution(mesh):
    in_specs = (P(None, "beam"), P(), P())
    out_specs = P(None, "grp", "beam")
    return jax.shard_map(local, mesh=mesh, in_specs=in_specs, out_specs=out_specs, check_vma=False)
```

```python
import math

import jax
import jax.numpy as jnp
import numpy as np
from jax import lax
from jax.experimental import pallas as pl
from jax.experimental.pallas import tpu as pltpu
from jax.sharding import PartitionSpec as P

G = 512
BAND = 256
NQ = 384
PHASE_SCALE = 2.5
CHIRP_RATE = 20
PEERS = 32
HALF = 256
HIGH = 96
ROWS = 12

F32 = jnp.float32
BF16 = jnp.bfloat16


def frequencies():
    reach = math.isqrt((G * G - 1) // 9)
    band = np.arange(-BAND // 2, BAND // 2)
    high = np.arange(BAND // 2, reach + 1)
    low = np.arange(-reach, -BAND // 2)
    return np.concatenate([band, high, low])


def forward_table(places):
    freqs = frequencies()
    phases = np.mod(freqs[None, :] * places[:, None], G)
    angle = 2.0 * np.pi / G * phases
    table = np.zeros((2, places.shape[0], NQ), np.float64)
    table[0, :, : freqs.size] = np.cos(angle) / np.sqrt(G)
    table[1, :, : freqs.size] = -np.sin(angle) / np.sqrt(G)
    return table


def constant_tables():
    places = np.arange(G)
    permuted = (4 * np.arange(G // 4)[None, :] + np.arange(4)[:, None]).reshape(-1)
    natural = forward_table(places)
    shuffled = forward_table(permuted)
    right = np.concatenate([natural[0], natural[1]], 1)
    runs = [slice(0, 128), slice(128, 256), slice(256, 256 + HIGH)]
    left = np.concatenate([shuffled[k][:, rows].T for rows in runs for k in range(2)], 0)
    back = np.concatenate([shuffled[0], -shuffled[1]], 1)
    freqs = frequencies()
    squared = np.full((NQ,), 1.0e9)
    squared[: freqs.size] = freqs * freqs
    angle = np.zeros((NQ,))
    angle[: freqs.size] = -2.0 * np.pi / (G * G) * np.mod(CHIRP_RATE * freqs * freqs, G * G)
    chirp = np.stack([np.cos(angle), np.sin(angle), squared], 0)
    lanes = np.zeros((8, NQ))
    lanes[:3] = chirp
    return (
        right.astype(BF16),
        left.astype(BF16),
        back.astype(BF16),
        lanes.astype(np.float32),
    )


def half_turn_fits():
    nodes = 0.5 * np.cos(np.pi * (np.arange(400) + 0.5) / 400)
    square = nodes * nodes
    root = math.sqrt(2.0)
    sine = root * np.sin(np.pi * nodes) / nodes
    cosine = root * np.cos(np.pi * nodes)
    fit = np.polynomial.Polynomial.fit
    return (
        [float(v) for v in fit(square, sine, 4, domain=[0, 0.25]).convert().coef],
        [float(v) for v in fit(square, cosine, 4, domain=[0, 0.25]).convert().coef],
    )


SINE, COSINE = half_turn_fits()


def horner(coefs, x):
    total = coefs[-1]
    for coef in coefs[-2::-1]:
        total = total * x + coef
    return total


def phase_factor(cells):
    turns = cells * (PHASE_SCALE / (2.0 * math.pi))
    rest = turns - jnp.round(turns)
    square = rest * rest
    sine = rest * horner(SINE, square)
    cosine = horner(COSINE, square)
    return 1.0 - sine * sine, sine * cosine


def own_core():
    return lax.axis_index("grp") % 2


def dot(a, b):
    return jnp.dot(a, b, preferred_element_type=F32)


def dot_t(a, b):
    return lax.dot_general(a, b, (((1,), (1,)), ((), ())), preferred_element_type=F32)


def prepare_kernel(beams, right, back, chirp, chirp_t, phi, prop, final):
    index = lax.broadcasted_iota(jnp.int32, (BAND, G), 0).astype(F32)
    on_x = index == beams[0:1, :]
    on_y = jnp.where(index == beams[1:2, :], 1.0, 0.0).astype(BF16)
    grid_r = dot_t(jnp.where(on_x, beams[2:3, :], 0.0).astype(BF16), on_y)
    grid_i = dot_t(jnp.where(on_x, beams[3:4, :], 0.0).astype(BF16), on_y)
    grid = jnp.concatenate([grid_r, grid_i], 1).astype(BF16)
    by_r = dot(back[:, 0:BAND], grid)
    by_i = dot(back[:, NQ : NQ + BAND], grid)
    mid_r = by_r[:, :BAND] - by_i[:, BAND:]
    mid_i = by_r[:, BAND:] + by_i[:, :BAND]
    band_r = right[:, 0:BAND]
    band_i = right[:, NQ : NQ + BAND]
    both = jnp.concatenate([band_r, band_i], 1)
    phi[:, :G] = dot_t(jnp.concatenate([mid_r, mid_i], 1).astype(BF16), both).astype(BF16)
    phi[:, G:] = dot_t(jnp.concatenate([mid_i, -mid_r], 1).astype(BF16), both).astype(BF16)
    inside = chirp_t[:, 2:3] + chirp[2:3, :] < (G * G - 1) // 9 + 0.5
    xr = chirp_t[:, 0:1]
    xi = chirp_t[:, 1:2]
    yr = chirp[0:1, :]
    yi = chirp[1:2, :]
    prop[:, :NQ] = jnp.where(inside, xr * yr - xi * yi, 0.0)
    prop[:, NQ:] = jnp.where(inside, xr * yi + xi * yr, 0.0)
    for h in range(2):
        rows = slice(h * HALF, h * HALF + HALF)
        top = slice(2 * h * HALF, (2 * h + 1) * HALF)
        low = slice((2 * h + 1) * HALF, (2 * h + 2) * HALF)
        final[top, :BAND] = right[rows, 0:BAND]
        final[top, BAND:] = right[rows, NQ : NQ + BAND]
        final[low, :BAND] = -right[rows, NQ : NQ + BAND]
        final[low, BAND:] = right[rows, 0:BAND]


def forward_rows(wide, phi, right, data, half, first, offset):
    for j in range(2):
        rows = slice(256 * j, 256 * j + 128)
        low = slice(256 * j + 128, 256 * j + 256)
        probe = pl.ds(pl.multiple_of(first + 128 * j, 128), 128)
        for h in range(4):
            cos, sin = phase_factor(wide[pl.ds(4 * j + h, 128, stride=ROWS), :])
            pr = phi[probe, 128 * h : 128 * h + 128].astype(F32)
            pi = phi[probe, G + 128 * h : G + 128 * h + 128].astype(F32)
            data[rows, 128 * h : 128 * h + 128] = (pr * cos - pi * sin).astype(BF16)
            data[low, 128 * h : 128 * h + 128] = (pr * sin + pi * cos).astype(BF16)
        both = dot(data[256 * j : 256 * j + 256, :], right[...])
        kept = pl.ds(pl.multiple_of(offset + 128 * j, 128), 128)
        half[kept, :NQ] = (both[:128, :NQ] - both[128:, NQ:]).astype(BF16)
        half[kept, NQ:] = (both[:128, NQ:] + both[128:, :NQ]).astype(BF16)


def second_factors(wide, factors, j):
    rows = slice(128 * j, 128 * j + 128)
    for q in range(2):
        cos, sin = phase_factor(wide[pl.ds(8 + 2 * j + q, 128, stride=ROWS), :])
        factors[rows, 128 * q : 128 * q + 128] = cos
        factors[rows, HALF + 128 * q : HALF + 128 * q + 128] = sin


def early_kernel(cells, phi, right, half, factors, wide, data):
    wide[...] = cells[...].astype(F32)
    forward_rows(wide, phi, right, data, half, own_core() * 256, 0)
    for j in range(2):
        second_factors(wide, factors, j)


def main_kernel(
    other, early, own_factors, right, phi, prop, back, left_far, out,
    wide, data, half, spec, fold, last, factors, rows_in, rows_out, left, sem,
):
    copy = pltpu.make_async_copy(left_far, left, sem)
    copy.start()
    place = lax.axis_index("beam")
    core = own_core()
    wide[...] = other[...].astype(F32)
    start = core * 256
    half[pl.ds(pl.multiple_of(start, 256), 256), :] = early[...]
    forward_rows(wide, phi, right, data, half, 256 - start, 256 - start)
    side = pl.ds(pl.multiple_of(place // 32 % 2 * HALF, HALF), HALF)
    copy.wait()
    for j in range(2):
        rows = slice(128 * j, 128 * j + 128)
        low = slice(NQ + 128 * j, NQ + 128 * j + 128)
        both = dot(left[256 * j : 256 * j + 256, :], half[...])
        second_factors(wide, factors, j)
        re = both[:128, :NQ] - both[128:, NQ:]
        im = both[:128, NQ:] + both[128:, :NQ]
        pr = prop[rows, :NQ]
        pi = prop[rows, NQ:]
        new_r = re * pr - im * pi
        new_i = re * pi + im * pr
        spec[256 * j : 256 * j + 128, :NQ] = new_r.astype(BF16)
        spec[256 * j : 256 * j + 128, NQ:] = new_i.astype(BF16)
        spec[256 * j + 128 : 256 * j + 256, :NQ] = new_i.astype(BF16)
        spec[256 * j + 128 : 256 * j + 256, NQ:] = (-new_r).astype(BF16)
        both = dot_t(spec[256 * j : 256 * j + 256, :], right[side, :])
        fold[rows, :HALF] = both[:128].astype(BF16)
        fold[rows, HALF:] = both[128:].astype(BF16)
        fold[low, :HALF] = (-both[128:]).astype(BF16)
        fold[low, HALF:] = both[:128].astype(BF16)
    rows = slice(256, 256 + HIGH)
    low = slice(NQ + 256, NQ + 256 + HIGH)
    one = dot(left[512 : 512 + 2 * HIGH, :], half[:, :BAND])
    two = dot(left[512 : 512 + 2 * HIGH, :], half[:, NQ : NQ + BAND])
    re = one[:HIGH] - two[HIGH:]
    im = two[:HIGH] + one[HIGH:]
    pr = prop[rows, :BAND]
    pi = prop[rows, NQ : NQ + BAND]
    new_r = re * pr - im * pi
    new_i = re * pi + im * pr
    one = jnp.concatenate([new_r, new_i], 0).astype(BF16)
    two = jnp.concatenate([new_i, -new_r], 0).astype(BF16)
    both = dot_t(one, right[side, :BAND]) + dot_t(two, right[side, NQ : NQ + BAND])
    fold[rows, :HALF] = both[:HIGH].astype(BF16)
    fold[rows, HALF:] = both[HIGH:].astype(BF16)
    fold[low, :HALF] = (-both[HIGH:]).astype(BF16)
    fold[low, HALF:] = both[:HIGH].astype(BF16)
    rest = jnp.zeros((NQ - 256 - HIGH, 2 * HALF), BF16)
    fold[256 + HIGH : NQ, :] = rest
    fold[NQ + 256 + HIGH :, :] = rest
    for table, first in ((factors, 256 - start), (own_factors, start)):
        rows = pl.ds(pl.multiple_of(first, 256), 256)
        wave = dot(back[rows, :], fold[...])
        cos = table[:, :HALF]
        sin = table[:, HALF:]
        last[rows, :HALF] = (wave[:, :HALF] * cos - wave[:, HALF:] * sin).astype(BF16)
        last[rows, HALF:] = (wave[:, :HALF] * sin + wave[:, HALF:] * cos).astype(BF16)
    both = dot(left[pl.ds(pl.multiple_of(place // 64 * 256, 256), 256), :], last[...])
    parts = (both[:128, :HALF] - both[128:, HALF:], both[:128, HALF:] + both[128:, :HALF])
    for q in range(4):
        rows_in[...] = parts[q // 2][:, 128 * (q % 2) : 128 * (q % 2) + 128]
        for row in range(2):
            own = rows_in[pl.ds(place % 2 * 2 + row, PEERS, stride=4), :]
            rows_out[pl.ds(2 * q + row, PEERS, stride=8), :] = own
    out[...] = rows_out[...].astype(BF16)


def final_kernel(parts, final, prop, out, wide, data):
    wide[...] = parts[...].astype(F32)
    for h in range(2):
        for q in range(4):
            for row in range(2):
                own = wide[pl.ds(128 * h + 2 * q + row, 16, stride=8), :]
                cols = slice(512 * h + 128 * q, 512 * h + 128 * q + 128)
                data[16 * row : 16 * row + 16, cols] = own.astype(BF16)
    acc = dot(data[...], final[...])
    for row in range(2):
        re = acc[16 * row : 16 * row + 16, :BAND]
        im = acc[16 * row : 16 * row + 16, BAND:]
        pr = prop[row : row + 1, :BAND]
        pi = prop[row : row + 1, BAND:]
        cols = slice(row * BAND, row * BAND + BAND)
        out[0, :, cols] = re * pr - im * pi
        out[1, :, cols] = re * pi + im * pr


VMEM = pl.BlockSpec(memory_space=pltpu.VMEM)
LIMIT = pltpu.CompilerParams(vmem_limit_bytes=16 * 1024 * 1024)
FAR = pl.BlockSpec(memory_space=pltpu.HBM)
placed = pltpu.with_memory_space_constraint


def prepare(beams, right, back, chirp):
    return pl.pallas_call(
        prepare_kernel,
        in_specs=[VMEM] * 5,
        out_specs=[VMEM] * 3,
        out_shape=[
            pltpu.VMEM((G, 2 * G), BF16),
            pltpu.HBM((NQ, 2 * NQ), F32),
            pltpu.VMEM((2 * G, 2 * BAND), BF16),
        ],
        compiler_params=LIMIT,
        name="prepare",
    )(beams, right, back, chirp, chirp.T)


def early(cells, phi, right):
    return pl.pallas_call(
        early_kernel,
        in_specs=[VMEM] * 3,
        out_specs=[VMEM] * 2,
        out_shape=[pltpu.VMEM((G // 2, 2 * NQ), BF16), pltpu.VMEM((G // 2, 2 * HALF), F32)],
        scratch_shapes=[
            pltpu.VMEM((cells.shape[0], 128), F32),
            pltpu.VMEM((G, G), BF16),
        ],
        compiler_params=LIMIT,
        name="early",
    )(cells, phi, right)


def main(near, left):
    rows = near[0].shape[0]
    return pl.pallas_call(
        main_kernel,
        in_specs=[VMEM] * 7 + [FAR],
        out_specs=VMEM,
        out_shape=jax.ShapeDtypeStruct((8 * PEERS, 128), BF16),
        scratch_shapes=[
            pltpu.VMEM((rows, 128), F32),
            pltpu.VMEM((G, G), BF16),
            pltpu.VMEM((G, 2 * NQ), BF16),
            pltpu.VMEM((512, 2 * NQ), BF16),
            pltpu.VMEM((2 * NQ, 2 * HALF), BF16),
            pltpu.VMEM((G, 2 * HALF), BF16),
            pltpu.VMEM((G // 2, 2 * HALF), F32),
            pltpu.VMEM((4 * PEERS, 128), F32),
            pltpu.VMEM((8 * PEERS, 128), F32),
            pltpu.VMEM(left.shape, BF16),
            pltpu.SemaphoreType.DMA,
        ],
        compiler_params=LIMIT,
        name="propagate",
    )(*near, left)


def finish(parts, final, prop):
    return pl.pallas_call(
        final_kernel,
        in_specs=[VMEM] * 3,
        out_specs=VMEM,
        out_shape=jax.ShapeDtypeStruct((2, 16, 2 * BAND), F32),
        scratch_shapes=[pltpu.VMEM((8 * PEERS, 128), F32), pltpu.VMEM((32, 1024), BF16)],
        compiler_params=LIMIT,
        name="finish",
    )(parts, final, prop)


def own_coefficients(vectors, site):
    wave_x = vectors[:, 0]
    wave_y = vectors[:, 1]
    phases = jnp.mod(site[0] * wave_x + site[1] * wave_y, G)
    angle = -2.0 * math.pi / G * phases.astype(F32)
    weight = jnp.exp(-(wave_x * wave_x + wave_y * wave_y).astype(F32) * (8.0 / (BAND * BAND)))
    weight = weight * (1.0 / math.sqrt(vectors.shape[0]))
    coef_r = (weight * jnp.cos(angle)).astype(BF16).astype(F32) * G
    coef_i = (weight * jnp.sin(angle)).astype(BF16).astype(F32) * G
    offset = BAND // 2
    rows = [(wave_x + offset).astype(F32), (wave_y + offset).astype(F32), coef_r, coef_i]
    return jnp.concatenate([jnp.stack(rows, 0), jnp.zeros((4, vectors.shape[0]), F32)], 0)


def band_rows(first):
    fx = first + jnp.arange(2, dtype=jnp.int32) - BAND // 2
    fy = jnp.arange(BAND, dtype=jnp.int32) - BAND // 2
    squared = fx[:, None] * fx[:, None] + fy[None, :] * fy[None, :]
    inside = (9 * squared < G * G).astype(F32)
    angle = -2.0 * math.pi / (G * G) * jnp.mod(CHIRP_RATE * squared, G * G).astype(F32)
    return jnp.concatenate([inside * jnp.cos(angle), inside * jnp.sin(angle)], 1)


def message_kernel(cells, out, rows, block):
    wide = cells[...].astype(F32)
    own = jnp.where(own_core() == 0, wide[:, : 2 * G], wide[:, 2 * G :])
    for k in range(8):
        rows[k : k + 1, :] = own[0:1, 128 * k : 128 * k + 128]
    size = 8 * ROWS
    for h in range(2):
        for k in range(4):
            at = G * (k // 2) + HALF * h + 128 * (k % 2)
            rows[8 + k : 9 + k, :] = own[1:2, at : at + 128]
        for m in range(8):
            block[ROWS * m : ROWS * m + ROWS, :] = rows[...]
        copies = block[...].astype(BF16)
        for t in range(16):
            if t // 4 % 2 == h:
                out[t * size : (t + 1) * size, :] = copies


def message(potential):
    return pl.pallas_call(
        message_kernel,
        in_specs=[VMEM],
        out_specs=VMEM,
        out_shape=jax.ShapeDtypeStruct((128 * ROWS, 128), BF16),
        scratch_shapes=[pltpu.VMEM((ROWS, 128), F32), pltpu.VMEM((8 * ROWS, 128), F32)],
        compiler_params=LIMIT,
        name="message",
    )(potential)


def near_groups(peers):
    groups = []
    for turn in range(2):
        for core in range(2):
            groups.append([4 * k + 2 * ((k + turn) % 2) + core for k in range(peers)])
    return groups


def local(potential, wave_vectors, probe_sites):
    right, left, back, chirp = (jnp.asarray(t) for t in constant_tables())
    peers = lax.axis_size("beam")
    position = lax.axis_index("beam")
    group = lax.axis_index("grp")
    mine = message(potential).reshape(peers, ROWS // 2, 2, 128)
    cells = lax.all_to_all(
        mine, ("beam", "grp"), 0, 0, tiled=True, axis_index_groups=near_groups(peers)
    )
    probe = position // 16 % 2 * 8 + position // 2 % 8
    site = lax.dynamic_index_in_dim(probe_sites, group * 16 + probe, 0, keepdims=False)
    beams = own_coefficients(wave_vectors, site)
    made = prepare(beams, right, back, chirp)
    band = band_rows(2 * position)
    cells, phi, prop, final, band = lax.optimization_barrier((cells, *made, band))
    cells = cells.reshape(peers * ROWS, 128)
    other = lax.ppermute(cells, "grp", [(0, 1), (1, 0), (2, 3), (3, 2)])
    cells, right_near, phi = (placed(a, pltpu.VMEM) for a in (cells, right, phi))
    first, factors = (placed(a, pltpu.VMEM) for a in early(cells, phi, right_near))
    other, prop, back = (placed(a, pltpu.VMEM) for a in (other, prop, back))
    near = (other, first, factors, right_near, phi, prop, back)
    sent = main(near, placed(left, pltpu.HBM))
    runs = [
        [64 * far + 16 * z + 2 * y + x for z in range(4) for y in range(8)]
        for far in range(2)
        for x in range(2)
    ]
    parts = lax.all_to_all(
        sent.reshape(PEERS, 8, 128), "beam", 0, 0, tiled=True, axis_index_groups=runs
    )
    return finish(parts.reshape(8 * PEERS, 128), placed(final, pltpu.VMEM), band)


def solution(mesh):
    in_specs = (P(None, "beam"), P(), P())
    out_specs = P(None, "grp", "beam")
    return jax.shard_map(local, mesh=mesh, in_specs=in_specs, out_specs=out_specs, check_vma=False)
```

```python
import math

import jax
import jax.numpy as jnp
import numpy as np
from jax import lax
from jax.experimental import pallas as pl
from jax.experimental.pallas import tpu as pltpu
from jax.sharding import PartitionSpec as P

G = 512
BAND = 256
NQ = 384
PHASE_SCALE = 2.5
CHIRP_RATE = 20
PEERS = 32
HALF = 256
HIGH = 96
ROWS = 12

F32 = jnp.float32
BF16 = jnp.bfloat16


def frequencies():
    reach = math.isqrt((G * G - 1) // 9)
    band = np.arange(-BAND // 2, BAND // 2)
    high = np.arange(BAND // 2, reach + 1)
    low = np.arange(-reach, -BAND // 2)
    return np.concatenate([band, high, low])


def forward_table(places):
    freqs = frequencies()
    phases = np.mod(freqs[None, :] * places[:, None], G)
    angle = 2.0 * np.pi / G * phases
    table = np.zeros((2, places.shape[0], NQ), np.float64)
    table[0, :, : freqs.size] = np.cos(angle) / np.sqrt(G)
    table[1, :, : freqs.size] = -np.sin(angle) / np.sqrt(G)
    return table


def constant_tables():
    places = np.arange(G)
    permuted = (4 * np.arange(G // 4)[None, :] + np.arange(4)[:, None]).reshape(-1)
    natural = forward_table(places)
    shuffled = forward_table(permuted)
    right = np.concatenate([natural[0], natural[1]], 1)
    runs = [slice(0, 128), slice(128, 256), slice(256, 256 + HIGH)]
    left = np.concatenate([shuffled[k][:, rows].T for rows in runs for k in range(2)], 0)
    back = np.concatenate([shuffled[0], -shuffled[1]], 1)
    freqs = frequencies()
    squared = np.full((NQ,), 1.0e9)
    squared[: freqs.size] = freqs * freqs
    angle = np.zeros((NQ,))
    angle[: freqs.size] = -2.0 * np.pi / (G * G) * np.mod(CHIRP_RATE * freqs * freqs, G * G)
    chirp = np.stack([np.cos(angle), np.sin(angle), squared], 0)
    lanes = np.zeros((8, NQ))
    lanes[:3] = chirp
    return (
        right.astype(BF16),
        left.astype(BF16),
        back.astype(BF16),
        lanes.astype(np.float32),
    )


def half_turn_fits():
    nodes = 0.5 * np.cos(np.pi * (np.arange(400) + 0.5) / 400)
    square = nodes * nodes
    root = math.sqrt(2.0)
    sine = root * np.sin(np.pi * nodes) / nodes
    cosine = root * np.cos(np.pi * nodes)
    fit = np.polynomial.Polynomial.fit
    return (
        [float(v) for v in fit(square, sine, 4, domain=[0, 0.25]).convert().coef],
        [float(v) for v in fit(square, cosine, 4, domain=[0, 0.25]).convert().coef],
    )


SINE, COSINE = half_turn_fits()


def horner(coefs, x):
    total = coefs[-1]
    for coef in coefs[-2::-1]:
        total = total * x + coef
    return total


def phase_factor(cells):
    turns = cells * (PHASE_SCALE / (2.0 * math.pi))
    rest = turns - jnp.round(turns)
    square = rest * rest
    sine = rest * horner(SINE, square)
    cosine = horner(COSINE, square)
    return 1.0 - sine * sine, sine * cosine


def own_core():
    return lax.axis_index("grp") % 2


def dot(a, b):
    return jnp.dot(a, b, preferred_element_type=F32)


def dot_t(a, b):
    return lax.dot_general(a, b, (((1,), (1,)), ((), ())), preferred_element_type=F32)


def prepare_kernel(beams, right, back, chirp, chirp_t, phi, prop, final):
    index = lax.broadcasted_iota(jnp.int32, (BAND, G), 0).astype(F32)
    on_x = index == beams[0:1, :]
    on_y = jnp.where(index == beams[1:2, :], 1.0, 0.0).astype(BF16)
    grid_r = dot_t(jnp.where(on_x, beams[2:3, :], 0.0).astype(BF16), on_y)
    grid_i = dot_t(jnp.where(on_x, beams[3:4, :], 0.0).astype(BF16), on_y)
    grid = jnp.concatenate([grid_r, grid_i], 1).astype(BF16)
    by_r = dot(back[:, 0:BAND], grid)
    by_i = dot(back[:, NQ : NQ + BAND], grid)
    mid_r = by_r[:, :BAND] - by_i[:, BAND:]
    mid_i = by_r[:, BAND:] + by_i[:, :BAND]
    band_r = right[:, 0:BAND]
    band_i = right[:, NQ : NQ + BAND]
    both = jnp.concatenate([band_r, band_i], 1)
    phi[:, :G] = dot_t(jnp.concatenate([mid_r, mid_i], 1).astype(BF16), both).astype(BF16)
    phi[:, G:] = dot_t(jnp.concatenate([mid_i, -mid_r], 1).astype(BF16), both).astype(BF16)
    inside = chirp_t[:, 2:3] + chirp[2:3, :] < (G * G - 1) // 9 + 0.5
    xr = chirp_t[:, 0:1]
    xi = chirp_t[:, 1:2]
    yr = chirp[0:1, :]
    yi = chirp[1:2, :]
    prop[:, :NQ] = jnp.where(inside, xr * yr - xi * yi, 0.0)
    prop[:, NQ:] = jnp.where(inside, xr * yi + xi * yr, 0.0)
    for h in range(2):
        rows = slice(h * HALF, h * HALF + HALF)
        top = slice(2 * h * HALF, (2 * h + 1) * HALF)
        low = slice((2 * h + 1) * HALF, (2 * h + 2) * HALF)
        final[top, :BAND] = right[rows, 0:BAND]
        final[top, BAND:] = right[rows, NQ : NQ + BAND]
        final[low, :BAND] = -right[rows, NQ : NQ + BAND]
        final[low, BAND:] = right[rows, 0:BAND]


def forward_rows(wide, phi, right, data, half, first, offset):
    for j in range(2):
        rows = slice(256 * j, 256 * j + 128)
        low = slice(256 * j + 128, 256 * j + 256)
        probe = pl.ds(pl.multiple_of(first + 128 * j, 128), 128)
        for h in range(4):
            cos, sin = phase_factor(wide[pl.ds(4 * j + h, 128, stride=ROWS), :])
            pr = phi[probe, 128 * h : 128 * h + 128].astype(F32)
            pi = phi[probe, G + 128 * h : G + 128 * h + 128].astype(F32)
            data[rows, 128 * h : 128 * h + 128] = (pr * cos - pi * sin).astype(BF16)
            data[low, 128 * h : 128 * h + 128] = (pr * sin + pi * cos).astype(BF16)
        both = dot(data[256 * j : 256 * j + 256, :], right[...])
        kept = pl.ds(pl.multiple_of(offset + 128 * j, 128), 128)
        half[kept, :NQ] = (both[:128, :NQ] - both[128:, NQ:]).astype(BF16)
        half[kept, NQ:] = (both[:128, NQ:] + both[128:, :NQ]).astype(BF16)


def second_factors(wide, factors, j):
    rows = slice(128 * j, 128 * j + 128)
    for q in range(2):
        cos, sin = phase_factor(wide[pl.ds(8 + 2 * j + q, 128, stride=ROWS), :])
        factors[rows, 128 * q : 128 * q + 128] = cos
        factors[rows, HALF + 128 * q : HALF + 128 * q + 128] = sin


def early_kernel(cells, phi, right, left_far, half, factors, left, wide, data, sem):
    copy = pltpu.make_async_copy(left_far, left, sem)
    copy.start()
    wide[...] = cells[...].astype(F32)
    forward_rows(wide, phi, right, data, half, own_core() * 256, 0)
    for j in range(2):
        second_factors(wide, factors, j)
    copy.wait()


def main_kernel(
    other, early, own_factors, right, phi, prop, back, left, out,
    wide, data, half, spec, fold, last, factors, rows_in, rows_out,
):
    place = lax.axis_index("beam")
    core = own_core()
    wide[...] = other[...].astype(F32)
    start = core * 256
    half[pl.ds(pl.multiple_of(start, 256), 256), :] = early[...]
    forward_rows(wide, phi, right, data, half, 256 - start, 256 - start)
    side = pl.ds(pl.multiple_of(place // 32 % 2 * HALF, HALF), HALF)
    for j in range(2):
        rows = slice(128 * j, 128 * j + 128)
        low = slice(NQ + 128 * j, NQ + 128 * j + 128)
        both = dot(left[256 * j : 256 * j + 256, :], half[...])
        second_factors(wide, factors, j)
        re = both[:128, :NQ] - both[128:, NQ:]
        im = both[:128, NQ:] + both[128:, :NQ]
        pr = prop[rows, :NQ]
        pi = prop[rows, NQ:]
        new_r = re * pr - im * pi
        new_i = re * pi + im * pr
        spec[256 * j : 256 * j + 128, :NQ] = new_r.astype(BF16)
        spec[256 * j : 256 * j + 128, NQ:] = new_i.astype(BF16)
        spec[256 * j + 128 : 256 * j + 256, :NQ] = new_i.astype(BF16)
        spec[256 * j + 128 : 256 * j + 256, NQ:] = (-new_r).astype(BF16)
        both = dot_t(spec[256 * j : 256 * j + 256, :], right[side, :])
        fold[rows, :HALF] = both[:128].astype(BF16)
        fold[rows, HALF:] = both[128:].astype(BF16)
        fold[low, :HALF] = (-both[128:]).astype(BF16)
        fold[low, HALF:] = both[:128].astype(BF16)
    rows = slice(256, 256 + HIGH)
    low = slice(NQ + 256, NQ + 256 + HIGH)
    one = dot(left[512 : 512 + 2 * HIGH, :], half[:, :BAND])
    two = dot(left[512 : 512 + 2 * HIGH, :], half[:, NQ : NQ + BAND])
    re = one[:HIGH] - two[HIGH:]
    im = two[:HIGH] + one[HIGH:]
    pr = prop[rows, :BAND]
    pi = prop[rows, NQ : NQ + BAND]
    new_r = re * pr - im * pi
    new_i = re * pi + im * pr
    one = jnp.concatenate([new_r, new_i], 0).astype(BF16)
    two = jnp.concatenate([new_i, -new_r], 0).astype(BF16)
    both = dot_t(one, right[side, :BAND]) + dot_t(two, right[side, NQ : NQ + BAND])
    fold[rows, :HALF] = both[:HIGH].astype(BF16)
    fold[rows, HALF:] = both[HIGH:].astype(BF16)
    fold[low, :HALF] = (-both[HIGH:]).astype(BF16)
    fold[low, HALF:] = both[:HIGH].astype(BF16)
    rest = jnp.zeros((NQ - 256 - HIGH, 2 * HALF), BF16)
    fold[256 + HIGH : NQ, :] = rest
    fold[NQ + 256 + HIGH :, :] = rest
    for table, first in ((factors, 256 - start), (own_factors, start)):
        rows = pl.ds(pl.multiple_of(first, 256), 256)
        wave = dot(back[rows, :], fold[...])
        cos = table[:, :HALF]
        sin = table[:, HALF:]
        last[rows, :HALF] = (wave[:, :HALF] * cos - wave[:, HALF:] * sin).astype(BF16)
        last[rows, HALF:] = (wave[:, :HALF] * sin + wave[:, HALF:] * cos).astype(BF16)
    both = dot(left[pl.ds(pl.multiple_of(place // 64 * 256, 256), 256), :], last[...])
    parts = (both[:128, :HALF] - both[128:, HALF:], both[:128, HALF:] + both[128:, :HALF])
    for q in range(4):
        rows_in[...] = parts[q // 2][:, 128 * (q % 2) : 128 * (q % 2) + 128]
        for row in range(2):
            own = rows_in[pl.ds(place % 2 * 2 + row, PEERS, stride=4), :]
            rows_out[pl.ds(2 * q + row, PEERS, stride=8), :] = own
    out[...] = rows_out[...].astype(BF16)


def final_kernel(parts, final, prop, out, wide, data):
    wide[...] = parts[...].astype(F32)
    for h in range(2):
        for q in range(4):
            for row in range(2):
                own = wide[pl.ds(128 * h + 2 * q + row, 16, stride=8), :]
                cols = slice(512 * h + 128 * q, 512 * h + 128 * q + 128)
                data[16 * row : 16 * row + 16, cols] = own.astype(BF16)
    acc = dot(data[...], final[...])
    for row in range(2):
        re = acc[16 * row : 16 * row + 16, :BAND]
        im = acc[16 * row : 16 * row + 16, BAND:]
        pr = prop[row : row + 1, :BAND]
        pi = prop[row : row + 1, BAND:]
        cols = slice(row * BAND, row * BAND + BAND)
        out[0, :, cols] = re * pr - im * pi
        out[1, :, cols] = re * pi + im * pr


VMEM = pl.BlockSpec(memory_space=pltpu.VMEM)
LIMIT = pltpu.CompilerParams(vmem_limit_bytes=16 * 1024 * 1024)
FAR = pl.BlockSpec(memory_space=pltpu.HBM)
placed = pltpu.with_memory_space_constraint


def prepare(beams, right, back, chirp):
    return pl.pallas_call(
        prepare_kernel,
        in_specs=[VMEM] * 5,
        out_specs=[VMEM] * 3,
        out_shape=[
            pltpu.VMEM((G, 2 * G), BF16),
            pltpu.HBM((NQ, 2 * NQ), F32),
            pltpu.VMEM((2 * G, 2 * BAND), BF16),
        ],
        compiler_params=LIMIT,
        name="prepare",
    )(beams, right, back, chirp, chirp.T)


def early(cells, phi, right, left):
    return pl.pallas_call(
        early_kernel,
        in_specs=[VMEM] * 3 + [FAR],
        out_specs=[VMEM] * 3,
        out_shape=[
            pltpu.VMEM((G // 2, 2 * NQ), BF16),
            pltpu.VMEM((G // 2, 2 * HALF), F32),
            pltpu.VMEM(left.shape, BF16),
        ],
        scratch_shapes=[
            pltpu.VMEM((cells.shape[0], 128), F32),
            pltpu.VMEM((G, G), BF16),
            pltpu.SemaphoreType.DMA,
        ],
        compiler_params=LIMIT,
        name="early",
    )(cells, phi, right, left)


def main(near):
    rows = near[0].shape[0]
    return pl.pallas_call(
        main_kernel,
        in_specs=[VMEM] * 8,
        out_specs=VMEM,
        out_shape=jax.ShapeDtypeStruct((8 * PEERS, 128), BF16),
        scratch_shapes=[
            pltpu.VMEM((rows, 128), F32),
            pltpu.VMEM((G, G), BF16),
            pltpu.VMEM((G, 2 * NQ), BF16),
            pltpu.VMEM((512, 2 * NQ), BF16),
            pltpu.VMEM((2 * NQ, 2 * HALF), BF16),
            pltpu.VMEM((G, 2 * HALF), BF16),
            pltpu.VMEM((G // 2, 2 * HALF), F32),
            pltpu.VMEM((4 * PEERS, 128), F32),
            pltpu.VMEM((8 * PEERS, 128), F32),
        ],
        compiler_params=LIMIT,
        name="propagate",
    )(*near)


def finish(parts, final, prop):
    return pl.pallas_call(
        final_kernel,
        in_specs=[VMEM] * 3,
        out_specs=VMEM,
        out_shape=jax.ShapeDtypeStruct((2, 16, 2 * BAND), F32),
        scratch_shapes=[pltpu.VMEM((8 * PEERS, 128), F32), pltpu.VMEM((32, 1024), BF16)],
        compiler_params=LIMIT,
        name="finish",
    )(parts, final, prop)


def own_coefficients(vectors, site):
    wave_x = vectors[:, 0]
    wave_y = vectors[:, 1]
    phases = jnp.mod(site[0] * wave_x + site[1] * wave_y, G)
    angle = -2.0 * math.pi / G * phases.astype(F32)
    weight = jnp.exp(-(wave_x * wave_x + wave_y * wave_y).astype(F32) * (8.0 / (BAND * BAND)))
    weight = weight * (1.0 / math.sqrt(vectors.shape[0]))
    coef_r = (weight * jnp.cos(angle)).astype(BF16).astype(F32) * G
    coef_i = (weight * jnp.sin(angle)).astype(BF16).astype(F32) * G
    offset = BAND // 2
    rows = [(wave_x + offset).astype(F32), (wave_y + offset).astype(F32), coef_r, coef_i]
    return jnp.concatenate([jnp.stack(rows, 0), jnp.zeros((4, vectors.shape[0]), F32)], 0)


def band_rows(first):
    fx = first + jnp.arange(2, dtype=jnp.int32) - BAND // 2
    fy = jnp.arange(BAND, dtype=jnp.int32) - BAND // 2
    squared = fx[:, None] * fx[:, None] + fy[None, :] * fy[None, :]
    inside = (9 * squared < G * G).astype(F32)
    angle = -2.0 * math.pi / (G * G) * jnp.mod(CHIRP_RATE * squared, G * G).astype(F32)
    return jnp.concatenate([inside * jnp.cos(angle), inside * jnp.sin(angle)], 1)


def message_kernel(cells, out, rows, block):
    wide = cells[...].astype(F32)
    own = jnp.where(own_core() == 0, wide[:, : 2 * G], wide[:, 2 * G :])
    for k in range(8):
        rows[k : k + 1, :] = own[0:1, 128 * k : 128 * k + 128]
    size = 8 * ROWS
    for h in range(2):
        for k in range(4):
            at = G * (k // 2) + HALF * h + 128 * (k % 2)
            rows[8 + k : 9 + k, :] = own[1:2, at : at + 128]
        for m in range(8):
            block[ROWS * m : ROWS * m + ROWS, :] = rows[...]
        copies = block[...].astype(BF16)
        for t in range(16):
            if t // 4 % 2 == h:
                out[t * size : (t + 1) * size, :] = copies


def message(potential):
    return pl.pallas_call(
        message_kernel,
        in_specs=[VMEM],
        out_specs=VMEM,
        out_shape=jax.ShapeDtypeStruct((128 * ROWS, 128), BF16),
        scratch_shapes=[pltpu.VMEM((ROWS, 128), F32), pltpu.VMEM((8 * ROWS, 128), F32)],
        compiler_params=LIMIT,
        name="message",
    )(potential)


def near_groups(peers):
    groups = []
    for turn in range(2):
        for core in range(2):
            groups.append([4 * k + 2 * ((k + turn) % 2) + core for k in range(peers)])
    return groups


def local(potential, wave_vectors, probe_sites):
    right, left, back, chirp = (jnp.asarray(t) for t in constant_tables())
    peers = lax.axis_size("beam")
    position = lax.axis_index("beam")
    group = lax.axis_index("grp")
    mine = message(potential).reshape(peers, ROWS // 2, 2, 128)
    cells = lax.all_to_all(
        mine, ("beam", "grp"), 0, 0, tiled=True, axis_index_groups=near_groups(peers)
    )
    probe = position // 16 % 2 * 8 + position // 2 % 8
    site = lax.dynamic_index_in_dim(probe_sites, group * 16 + probe, 0, keepdims=False)
    beams = own_coefficients(wave_vectors, site)
    made = prepare(beams, right, back, chirp)
    band = band_rows(2 * position)
    cells, phi, prop, final, band = lax.optimization_barrier((cells, *made, band))
    cells = cells.reshape(peers * ROWS, 128)
    other = lax.ppermute(cells, "grp", [(0, 1), (1, 0), (2, 3), (3, 2)])
    cells, right_near, phi = (placed(a, pltpu.VMEM) for a in (cells, right, phi))
    made = early(cells, phi, right_near, placed(left, pltpu.HBM))
    first, factors, left = (placed(a, pltpu.VMEM) for a in made)
    other, prop, back = (placed(a, pltpu.VMEM) for a in (other, prop, back))
    sent = main((other, first, factors, right_near, phi, prop, back, left))
    runs = [
        [64 * far + 16 * z + 2 * y + x for z in range(4) for y in range(8)]
        for far in range(2)
        for x in range(2)
    ]
    parts = lax.all_to_all(
        sent.reshape(PEERS, 8, 128), "beam", 0, 0, tiled=True, axis_index_groups=runs
    )
    return finish(parts.reshape(8 * PEERS, 128), placed(final, pltpu.VMEM), band)


def solution(mesh):
    in_specs = (P(None, "beam"), P(), P())
    out_specs = P(None, "grp", "beam")
    return jax.shard_map(local, mesh=mesh, in_specs=in_specs, out_specs=out_specs, check_vma=False)
```

```python
import math

import jax
import jax.numpy as jnp
import numpy as np
from jax import lax
from jax.experimental import pallas as pl
from jax.experimental.pallas import tpu as pltpu
from jax.sharding import PartitionSpec as P

G = 512
BAND = 256
NQ = 384
PHASE_SCALE = 2.5
CHIRP_RATE = 20
PEERS = 32
HALF = 256
HIGH = 96
ROWS = 12

F32 = jnp.float32
BF16 = jnp.bfloat16


def frequencies():
    reach = math.isqrt((G * G - 1) // 9)
    band = np.arange(-BAND // 2, BAND // 2)
    high = np.arange(BAND // 2, reach + 1)
    low = np.arange(-reach, -BAND // 2)
    return np.concatenate([band, high, low])


def forward_table(places):
    freqs = frequencies()
    phases = np.mod(freqs[None, :] * places[:, None], G)
    angle = 2.0 * np.pi / G * phases
    table = np.zeros((2, places.shape[0], NQ), np.float64)
    table[0, :, : freqs.size] = np.cos(angle) / np.sqrt(G)
    table[1, :, : freqs.size] = -np.sin(angle) / np.sqrt(G)
    return table


def constant_tables():
    places = np.arange(G)
    permuted = (4 * np.arange(G // 4)[None, :] + np.arange(4)[:, None]).reshape(-1)
    natural = forward_table(places)
    shuffled = forward_table(permuted)
    right = np.concatenate([natural[0], natural[1]], 1)
    runs = [slice(0, 128), slice(128, 256), slice(256, 256 + HIGH)]
    left = np.concatenate([shuffled[k][:, rows].T for rows in runs for k in range(2)], 0)
    back = np.concatenate([shuffled[0], -shuffled[1]], 1)
    freqs = frequencies()
    squared = np.full((NQ,), 1.0e9)
    squared[: freqs.size] = freqs * freqs
    angle = np.zeros((NQ,))
    angle[: freqs.size] = -2.0 * np.pi / (G * G) * np.mod(CHIRP_RATE * freqs * freqs, G * G)
    chirp = np.stack([np.cos(angle), np.sin(angle), squared], 0)
    lanes = np.zeros((8, NQ))
    lanes[:3] = chirp
    return (
        right.astype(BF16),
        left.astype(BF16),
        back.astype(BF16),
        lanes.astype(np.float32),
    )


def half_turn_fits():
    nodes = 0.5 * np.cos(np.pi * (np.arange(400) + 0.5) / 400)
    square = nodes * nodes
    root = math.sqrt(2.0)
    sine = root * np.sin(np.pi * nodes) / nodes
    cosine = root * np.cos(np.pi * nodes)
    fit = np.polynomial.Polynomial.fit
    return (
        [float(v) for v in fit(square, sine, 4, domain=[0, 0.25]).convert().coef],
        [float(v) for v in fit(square, cosine, 4, domain=[0, 0.25]).convert().coef],
    )


SINE, COSINE = half_turn_fits()


def horner(coefs, x):
    total = coefs[-1]
    for coef in coefs[-2::-1]:
        total = total * x + coef
    return total


def phase_factor(cells):
    turns = cells * (PHASE_SCALE / (2.0 * math.pi))
    rest = turns - jnp.round(turns)
    square = rest * rest
    sine = rest * horner(SINE, square)
    cosine = horner(COSINE, square)
    return 1.0 - sine * sine, sine * cosine


def own_core():
    return lax.axis_index("grp") % 2


def dot(a, b):
    return jnp.dot(a, b, preferred_element_type=F32)


def dot_t(a, b):
    return lax.dot_general(a, b, (((1,), (1,)), ((), ())), preferred_element_type=F32)


def prepare_kernel(
    beams, right_far, back_far, chirp, chirp_t, phi, prop, final, right, back, sems
):
    copies = (
        pltpu.make_async_copy(right_far, right, sems.at[0]),
        pltpu.make_async_copy(back_far, back, sems.at[1]),
    )
    for copy in copies:
        copy.start()
    for copy in copies:
        copy.wait()
    index = lax.broadcasted_iota(jnp.int32, (BAND, G), 0).astype(F32)
    on_x = index == beams[0:1, :]
    on_y = jnp.where(index == beams[1:2, :], 1.0, 0.0).astype(BF16)
    grid_r = dot_t(jnp.where(on_x, beams[2:3, :], 0.0).astype(BF16), on_y)
    grid_i = dot_t(jnp.where(on_x, beams[3:4, :], 0.0).astype(BF16), on_y)
    grid = jnp.concatenate([grid_r, grid_i], 1).astype(BF16)
    by_r = dot(back[:, 0:BAND], grid)
    by_i = dot(back[:, NQ : NQ + BAND], grid)
    mid_r = by_r[:, :BAND] - by_i[:, BAND:]
    mid_i = by_r[:, BAND:] + by_i[:, :BAND]
    band_r = right[:, 0:BAND]
    band_i = right[:, NQ : NQ + BAND]
    both = jnp.concatenate([band_r, band_i], 1)
    phi[:, :G] = dot_t(jnp.concatenate([mid_r, mid_i], 1).astype(BF16), both).astype(BF16)
    phi[:, G:] = dot_t(jnp.concatenate([mid_i, -mid_r], 1).astype(BF16), both).astype(BF16)
    inside = chirp_t[:, 2:3] + chirp[2:3, :] < (G * G - 1) // 9 + 0.5
    xr = chirp_t[:, 0:1]
    xi = chirp_t[:, 1:2]
    yr = chirp[0:1, :]
    yi = chirp[1:2, :]
    prop[:, :NQ] = jnp.where(inside, xr * yr - xi * yi, 0.0)
    prop[:, NQ:] = jnp.where(inside, xr * yi + xi * yr, 0.0)
    for h in range(2):
        rows = slice(h * HALF, h * HALF + HALF)
        top = slice(2 * h * HALF, (2 * h + 1) * HALF)
        low = slice((2 * h + 1) * HALF, (2 * h + 2) * HALF)
        final[top, :BAND] = right[rows, 0:BAND]
        final[top, BAND:] = right[rows, NQ : NQ + BAND]
        final[low, :BAND] = -right[rows, NQ : NQ + BAND]
        final[low, BAND:] = right[rows, 0:BAND]


def forward_rows(wide, phi, right, data, half, first, offset):
    for j in range(2):
        rows = slice(256 * j, 256 * j + 128)
        low = slice(256 * j + 128, 256 * j + 256)
        probe = pl.ds(pl.multiple_of(first + 128 * j, 128), 128)
        for h in range(4):
            cos, sin = phase_factor(wide[pl.ds(4 * j + h, 128, stride=ROWS), :])
            pr = phi[probe, 128 * h : 128 * h + 128].astype(F32)
            pi = phi[probe, G + 128 * h : G + 128 * h + 128].astype(F32)
            data[rows, 128 * h : 128 * h + 128] = (pr * cos - pi * sin).astype(BF16)
            data[low, 128 * h : 128 * h + 128] = (pr * sin + pi * cos).astype(BF16)
        both = dot(data[256 * j : 256 * j + 256, :], right[...])
        kept = pl.ds(pl.multiple_of(offset + 128 * j, 128), 128)
        half[kept, :NQ] = (both[:128, :NQ] - both[128:, NQ:]).astype(BF16)
        half[kept, NQ:] = (both[:128, NQ:] + both[128:, :NQ]).astype(BF16)


def second_factors(wide, factors, j):
    rows = slice(128 * j, 128 * j + 128)
    for q in range(2):
        cos, sin = phase_factor(wide[pl.ds(8 + 2 * j + q, 128, stride=ROWS), :])
        factors[rows, 128 * q : 128 * q + 128] = cos
        factors[rows, HALF + 128 * q : HALF + 128 * q + 128] = sin


def early_kernel(cells, phi, right, left_far, half, factors, left, wide, data, sem):
    copy = pltpu.make_async_copy(left_far, left, sem)
    copy.start()
    wide[...] = cells[...].astype(F32)
    forward_rows(wide, phi, right, data, half, own_core() * 256, 0)
    for j in range(2):
        second_factors(wide, factors, j)
    copy.wait()


def main_kernel(
    other, early, own_factors, right, phi, prop, back, left, out,
    wide, data, half, spec, fold, last, factors, rows_in, rows_out,
):
    place = lax.axis_index("beam")
    core = own_core()
    wide[...] = other[...].astype(F32)
    start = core * 256
    half[pl.ds(pl.multiple_of(start, 256), 256), :] = early[...]
    forward_rows(wide, phi, right, data, half, 256 - start, 256 - start)
    side = pl.ds(pl.multiple_of(place // 32 % 2 * HALF, HALF), HALF)
    for j in range(2):
        rows = slice(128 * j, 128 * j + 128)
        low = slice(NQ + 128 * j, NQ + 128 * j + 128)
        both = dot(left[256 * j : 256 * j + 256, :], half[...])
        second_factors(wide, factors, j)
        re = both[:128, :NQ] - both[128:, NQ:]
        im = both[:128, NQ:] + both[128:, :NQ]
        pr = prop[rows, :NQ]
        pi = prop[rows, NQ:]
        new_r = re * pr - im * pi
        new_i = re * pi + im * pr
        spec[256 * j : 256 * j + 128, :NQ] = new_r.astype(BF16)
        spec[256 * j : 256 * j + 128, NQ:] = new_i.astype(BF16)
        spec[256 * j + 128 : 256 * j + 256, :NQ] = new_i.astype(BF16)
        spec[256 * j + 128 : 256 * j + 256, NQ:] = (-new_r).astype(BF16)
        both = dot_t(spec[256 * j : 256 * j + 256, :], right[side, :])
        fold[rows, :HALF] = both[:128].astype(BF16)
        fold[rows, HALF:] = both[128:].astype(BF16)
        fold[low, :HALF] = (-both[128:]).astype(BF16)
        fold[low, HALF:] = both[:128].astype(BF16)
    rows = slice(256, 256 + HIGH)
    low = slice(NQ + 256, NQ + 256 + HIGH)
    one = dot(left[512 : 512 + 2 * HIGH, :], half[:, :BAND])
    two = dot(left[512 : 512 + 2 * HIGH, :], half[:, NQ : NQ + BAND])
    re = one[:HIGH] - two[HIGH:]
    im = two[:HIGH] + one[HIGH:]
    pr = prop[rows, :BAND]
    pi = prop[rows, NQ : NQ + BAND]
    new_r = re * pr - im * pi
    new_i = re * pi + im * pr
    one = jnp.concatenate([new_r, new_i], 0).astype(BF16)
    two = jnp.concatenate([new_i, -new_r], 0).astype(BF16)
    both = dot_t(one, right[side, :BAND]) + dot_t(two, right[side, NQ : NQ + BAND])
    fold[rows, :HALF] = both[:HIGH].astype(BF16)
    fold[rows, HALF:] = both[HIGH:].astype(BF16)
    fold[low, :HALF] = (-both[HIGH:]).astype(BF16)
    fold[low, HALF:] = both[:HIGH].astype(BF16)
    rest = jnp.zeros((NQ - 256 - HIGH, 2 * HALF), BF16)
    fold[256 + HIGH : NQ, :] = rest
    fold[NQ + 256 + HIGH :, :] = rest
    for table, first in ((factors, 256 - start), (own_factors, start)):
        rows = pl.ds(pl.multiple_of(first, 256), 256)
        wave = dot(back[rows, :], fold[...])
        cos = table[:, :HALF]
        sin = table[:, HALF:]
        last[rows, :HALF] = (wave[:, :HALF] * cos - wave[:, HALF:] * sin).astype(BF16)
        last[rows, HALF:] = (wave[:, :HALF] * sin + wave[:, HALF:] * cos).astype(BF16)
    both = dot(left[pl.ds(pl.multiple_of(place // 64 * 256, 256), 256), :], last[...])
    parts = (both[:128, :HALF] - both[128:, HALF:], both[:128, HALF:] + both[128:, :HALF])
    for q in range(4):
        rows_in[...] = parts[q // 2][:, 128 * (q % 2) : 128 * (q % 2) + 128]
        for row in range(2):
            own = rows_in[pl.ds(place % 2 * 2 + row, PEERS, stride=4), :]
            rows_out[pl.ds(2 * q + row, PEERS, stride=8), :] = own
    out[...] = rows_out[...].astype(BF16)


def final_kernel(parts, final, prop, out, wide, data):
    wide[...] = parts[...].astype(F32)
    for h in range(2):
        for q in range(4):
            for row in range(2):
                own = wide[pl.ds(128 * h + 2 * q + row, 16, stride=8), :]
                cols = slice(512 * h + 128 * q, 512 * h + 128 * q + 128)
                data[16 * row : 16 * row + 16, cols] = own.astype(BF16)
    acc = dot(data[...], final[...])
    for row in range(2):
        re = acc[16 * row : 16 * row + 16, :BAND]
        im = acc[16 * row : 16 * row + 16, BAND:]
        pr = prop[row : row + 1, :BAND]
        pi = prop[row : row + 1, BAND:]
        cols = slice(row * BAND, row * BAND + BAND)
        out[0, :, cols] = re * pr - im * pi
        out[1, :, cols] = re * pi + im * pr


VMEM = pl.BlockSpec(memory_space=pltpu.VMEM)
LIMIT = pltpu.CompilerParams(vmem_limit_bytes=16 * 1024 * 1024)
FAR = pl.BlockSpec(memory_space=pltpu.HBM)
placed = pltpu.with_memory_space_constraint


def prepare(beams, right, back, chirp):
    return pl.pallas_call(
        prepare_kernel,
        in_specs=[VMEM, FAR, FAR, VMEM, VMEM],
        out_specs=[VMEM] * 4,
        out_shape=[
            pltpu.VMEM((G, 2 * G), BF16),
            pltpu.HBM((NQ, 2 * NQ), F32),
            pltpu.VMEM((2 * G, 2 * BAND), BF16),
            pltpu.VMEM(right.shape, BF16),
        ],
        scratch_shapes=[pltpu.VMEM(back.shape, BF16), pltpu.SemaphoreType.DMA((2,))],
        compiler_params=LIMIT,
        name="prepare",
    )(beams, placed(right, pltpu.HBM), placed(back, pltpu.HBM), chirp, chirp.T)


def early(cells, phi, right, left):
    return pl.pallas_call(
        early_kernel,
        in_specs=[VMEM] * 3 + [FAR],
        out_specs=[VMEM] * 3,
        out_shape=[
            pltpu.VMEM((G // 2, 2 * NQ), BF16),
            pltpu.VMEM((G // 2, 2 * HALF), F32),
            pltpu.VMEM(left.shape, BF16),
        ],
        scratch_shapes=[
            pltpu.VMEM((cells.shape[0], 128), F32),
            pltpu.VMEM((G, G), BF16),
            pltpu.SemaphoreType.DMA,
        ],
        compiler_params=LIMIT,
        name="early",
    )(cells, phi, right, left)


def main(near):
    rows = near[0].shape[0]
    return pl.pallas_call(
        main_kernel,
        in_specs=[VMEM] * 8,
        out_specs=VMEM,
        out_shape=jax.ShapeDtypeStruct((8 * PEERS, 128), BF16),
        scratch_shapes=[
            pltpu.VMEM((rows, 128), F32),
            pltpu.VMEM((G, G), BF16),
            pltpu.VMEM((G, 2 * NQ), BF16),
            pltpu.VMEM((512, 2 * NQ), BF16),
            pltpu.VMEM((2 * NQ, 2 * HALF), BF16),
            pltpu.VMEM((G, 2 * HALF), BF16),
            pltpu.VMEM((G // 2, 2 * HALF), F32),
            pltpu.VMEM((4 * PEERS, 128), F32),
            pltpu.VMEM((8 * PEERS, 128), F32),
        ],
        compiler_params=LIMIT,
        name="propagate",
    )(*near)


def finish(parts, final, prop):
    return pl.pallas_call(
        final_kernel,
        in_specs=[VMEM] * 3,
        out_specs=VMEM,
        out_shape=jax.ShapeDtypeStruct((2, 16, 2 * BAND), F32),
        scratch_shapes=[pltpu.VMEM((8 * PEERS, 128), F32), pltpu.VMEM((32, 1024), BF16)],
        compiler_params=LIMIT,
        name="finish",
    )(parts, final, prop)


def own_coefficients(vectors, site):
    wave_x = vectors[:, 0]
    wave_y = vectors[:, 1]
    phases = jnp.mod(site[0] * wave_x + site[1] * wave_y, G)
    angle = -2.0 * math.pi / G * phases.astype(F32)
    weight = jnp.exp(-(wave_x * wave_x + wave_y * wave_y).astype(F32) * (8.0 / (BAND * BAND)))
    weight = weight * (1.0 / math.sqrt(vectors.shape[0]))
    coef_r = (weight * jnp.cos(angle)).astype(BF16).astype(F32) * G
    coef_i = (weight * jnp.sin(angle)).astype(BF16).astype(F32) * G
    offset = BAND // 2
    rows = [(wave_x + offset).astype(F32), (wave_y + offset).astype(F32), coef_r, coef_i]
    return jnp.concatenate([jnp.stack(rows, 0), jnp.zeros((4, vectors.shape[0]), F32)], 0)


def band_rows(first):
    fx = first + jnp.arange(2, dtype=jnp.int32) - BAND // 2
    fy = jnp.arange(BAND, dtype=jnp.int32) - BAND // 2
    squared = fx[:, None] * fx[:, None] + fy[None, :] * fy[None, :]
    inside = (9 * squared < G * G).astype(F32)
    angle = -2.0 * math.pi / (G * G) * jnp.mod(CHIRP_RATE * squared, G * G).astype(F32)
    return jnp.concatenate([inside * jnp.cos(angle), inside * jnp.sin(angle)], 1)


def message_kernel(cells, out, rows, block):
    wide = cells[...].astype(F32)
    own = jnp.where(own_core() == 0, wide[:, : 2 * G], wide[:, 2 * G :])
    for k in range(8):
        rows[k : k + 1, :] = own[0:1, 128 * k : 128 * k + 128]
    size = 8 * ROWS
    for h in range(2):
        for k in range(4):
            at = G * (k // 2) + HALF * h + 128 * (k % 2)
            rows[8 + k : 9 + k, :] = own[1:2, at : at + 128]
        for m in range(8):
            block[ROWS * m : ROWS * m + ROWS, :] = rows[...]
        copies = block[...].astype(BF16)
        for t in range(16):
            if t // 4 % 2 == h:
                out[t * size : (t + 1) * size, :] = copies


def message(potential):
    return pl.pallas_call(
        message_kernel,
        in_specs=[VMEM],
        out_specs=VMEM,
        out_shape=jax.ShapeDtypeStruct((128 * ROWS, 128), BF16),
        scratch_shapes=[pltpu.VMEM((ROWS, 128), F32), pltpu.VMEM((8 * ROWS, 128), F32)],
        compiler_params=LIMIT,
        name="message",
    )(potential)


def near_groups(peers):
    groups = []
    for turn in range(2):
        for core in range(2):
            groups.append([4 * k + 2 * ((k + turn) % 2) + core for k in range(peers)])
    return groups


def local(potential, wave_vectors, probe_sites):
    right, left, back, chirp = (jnp.asarray(t) for t in constant_tables())
    peers = lax.axis_size("beam")
    position = lax.axis_index("beam")
    group = lax.axis_index("grp")
    mine = message(potential).reshape(peers, ROWS // 2, 2, 128)
    cells = lax.all_to_all(
        mine, ("beam", "grp"), 0, 0, tiled=True, axis_index_groups=near_groups(peers)
    )
    probe = position // 16 % 2 * 8 + position // 2 % 8
    site = lax.dynamic_index_in_dim(probe_sites, group * 16 + probe, 0, keepdims=False)
    beams = own_coefficients(wave_vectors, site)
    made = prepare(beams, right, back, chirp)
    band = band_rows(2 * position)
    cells, phi, prop, final, right, band = lax.optimization_barrier((cells, *made, band))
    cells = cells.reshape(peers * ROWS, 128)
    other = lax.ppermute(cells, "grp", [(0, 1), (1, 0), (2, 3), (3, 2)])
    cells, right_near, phi = (placed(a, pltpu.VMEM) for a in (cells, right, phi))
    made = early(cells, phi, right_near, placed(left, pltpu.HBM))
    first, factors, left = (placed(a, pltpu.VMEM) for a in made)
    other, prop, back = (placed(a, pltpu.VMEM) for a in (other, prop, back))
    sent = main((other, first, factors, right_near, phi, prop, back, left))
    runs = [
        [64 * far + 16 * z + 2 * y + x for z in range(4) for y in range(8)]
        for far in range(2)
        for x in range(2)
    ]
    parts = lax.all_to_all(
        sent.reshape(PEERS, 8, 128), "beam", 0, 0, tiled=True, axis_index_groups=runs
    )
    return finish(parts.reshape(8 * PEERS, 128), placed(final, pltpu.VMEM), band)


def solution(mesh):
    in_specs = (P(None, "beam"), P(), P())
    out_specs = P(None, "grp", "beam")
    return jax.shard_map(local, mesh=mesh, in_specs=in_specs, out_specs=out_specs, check_vma=False)
```
